128 devices in a mesh: wide: 32 (over y, z, core), narrow: 4 (over x).
Axes of the slice: x: 4, y: 4, z: 4, core: 2. Of those that a mesh axis runs over, the one named last changes fastest.
Arguments:
- charges: float32 [2, 8388608], P(None, ('wide', 'narrow')), may hold values from -6 to 6
- source_order: int32 [8388608], P(('wide', 'narrow')), may hold values from 0 to 7, as said below
- velocity: bfloat16 [1048576], P(('wide', 'narrow')), may hold values from 0.5 to 4
- leaf_weight: bfloat16 [16, 128], replicated, may hold values from -1.5 to 1.5
- mixing: bfloat16 [10, 2, 2, 128, 128], replicated, may hold values from -0.375 to 0.375
- eval_weight: bfloat16 [128, 16], replicated, may hold values from -0.5 to 0.5
- target_order: int32 [8388608], P(('wide', 'narrow')), may hold values from 0 to 7, as said below
Outputs:
- potentials: float32 [2, 8388608], P(None, ('wide', 'narrow'))
The draws below stay inside these ranges and needn't reach their ends.
Inputs may be any that keep to these rules, and one draw needn't show every extreme that they name: `source_order`: each aligned block of 8 entries is a permutation of 0 .. 7. `target_order`: each aligned block of 8 entries is a permutation of 0 .. 7.
All inputs are finite; a program needn't handle non-finite values.
Results may differ from the reference program's by a relative error of at most 0.02.
Values may be sent and summed in bfloat16 or wider, within the bound.
A program may use at most 128 MiB of HBM per device.

```python
import math
import jax
import jax.numpy as jnp

WIDTH = 128
LEAF = 8
BOX = 8192
LOCAL_LEVELS = 3
LEVELS = 10
NBOX = 1048576
NSRC = 8388608


def block_permutation(seed_key, blocks, length):
    scores = jax.random.randint(seed_key, (blocks, length), 0, 1 << 20, dtype=jnp.int32)
    scores = scores * length + jnp.arange(length, dtype=jnp.int32)[None, :]
    return jnp.argsort(scores, axis=1, stable=True).reshape(-1).astype(jnp.int32)


def draw_source_order(key, part):
    return block_permutation(jax.random.fold_in(key, 11), NSRC // LEAF, LEAF)


def draw_target_order(key, part):
    return block_permutation(jax.random.fold_in(key, 29), NSRC // LEAF, LEAF)


def levels(own_key, shape, split, low, largest):
    factor_of = 1.0
    for position, shards_of in split:
        steps = jax.random.uniform(jax.random.fold_in(jax.random.fold_in(own_key, 6), position), (shards_of,), jnp.float32, low / len(split), largest / len(split))
        factor_of = factor_of * jnp.repeat(jnp.exp(steps), shape[position] // shards_of).reshape((-1,) + (1,) * (len(shape) - 1 - position))
    return factor_of


def centred(own_key, shape, spread, limit, cuts=(), kind=jnp.bfloat16):
    factor_of = levels(own_key, shape, cuts, -0.22, 0.18) if cuts else 1.0
    result = jax.random.normal(own_key, shape, jnp.float32) * spread * factor_of
    return jnp.minimum(jnp.maximum(result, -limit), limit).astype(kind)


def setup_inputs(seed: int = 0) -> dict:
    streams_of = jax.random.split(jax.random.key(seed), 8)
    charges = centred(streams_of[0], (2, NSRC), 1.0, 6.0, ((1, 128),), jnp.float32)
    source_order = draw_source_order(jax.random.fold_in(streams_of[7], 71), 0)
    velocity = jnp.clip(jnp.exp(math.log(4.0) - 2.0794415 * jax.random.uniform(streams_of[2], (NBOX,), jnp.float32) ** levels(streams_of[2], (NBOX,), ((0, 128),), -0.2, 0.2)), 0.5, 4.0).astype(jnp.bfloat16)
    leaf_weight = centred(streams_of[3], (2 * LEAF, WIDTH), (2 * LEAF) ** -0.5, 1.5)
    mixing = centred(streams_of[4], (LEVELS, 2, 2, WIDTH, WIDTH), (2 * WIDTH) ** -0.5, 0.375)
    eval_weight = centred(streams_of[5], (WIDTH, 2 * LEAF), WIDTH ** -0.5, 0.5)
    target_order = draw_target_order(jax.random.fold_in(streams_of[7], 71), 0)
    return dict(charges=charges, source_order=source_order, velocity=velocity, leaf_weight=leaf_weight, mixing=mixing, eval_weight=eval_weight, target_order=target_order)


def rotate(pre, speeds, section_no):
    rank = pre.shape[1] // 2
    nodes = jnp.cos(math.pi * (jnp.arange(rank, dtype=jnp.float32) + 0.5) / rank)
    theta = (math.pi * (section_no + 1)) * speeds.astype(jnp.float32)[:, None] * nodes[None, :]
    cosine = jnp.cos(theta)
    sine = jnp.sin(theta)
    real_part = pre[:, :rank]
    imag_part = pre[:, rank:]
    return jnp.concatenate([real_part * cosine - imag_part * sine, real_part * sine + imag_part * cosine], axis=1).astype(jnp.bfloat16)


def butterfly_section(state, speeds, mixing, section_no, stride):
    total, width = state.shape
    blocks = state.reshape(total // (2 * stride), 2, stride, width)
    first = blocks[:, 0].reshape(-1, width)
    second = blocks[:, 1].reshape(-1, width)
    results = []
    for target in range(2):
        pre = jnp.dot(first, mixing[section_no, target, 0], preferred_element_type=jnp.float32)
        pre = pre + jnp.dot(second, mixing[section_no, target, 1], preferred_element_type=jnp.float32)
        results.append(pre.reshape(total // (2 * stride), stride, width))
    pre = jnp.stack(results, axis=1).reshape(total, width)
    return rotate(pre, speeds, section_no)


def reference(charges, source_order, velocity, leaf_weight, mixing, eval_weight, target_order):
    offsets = (jnp.arange(NSRC, dtype=jnp.int32) // LEAF) * LEAF
    ordered = jnp.take(charges, source_order.astype(jnp.int32) + offsets, axis=1)
    leaf_in = ordered.reshape(2, NBOX, LEAF).transpose(1, 0, 2).reshape(NBOX, 2 * LEAF).astype(jnp.bfloat16)
    state = jnp.dot(leaf_in, leaf_weight, preferred_element_type=jnp.float32).astype(jnp.bfloat16)
    box_bits = int(BOX).bit_length() - 1
    for section_no in range(LEVELS):
        if section_no < LOCAL_LEVELS:
            bit_no = section_no
        else:
            bit_no = box_bits + section_no - LOCAL_LEVELS
        state = butterfly_section(state, velocity, mixing, section_no, 2 ** bit_no)
    values = jnp.dot(state, eval_weight, preferred_element_type=jnp.float32)
    field = values.reshape(NBOX, 2, LEAF).transpose(1, 0, 2).reshape(2, NSRC)
    return jnp.take(field, target_order.astype(jnp.int32) + offsets, axis=1)
```

```python
import functools
import math

import jax
import jax.numpy as jnp
import numpy as np
from jax import lax
from jax.experimental import pallas as pl
from jax.experimental.pallas import tpu as pltpu
from jax.sharding import PartitionSpec as P

MESH = pl.DeviceIdType.MESH
LEVELS = 10
PARTS = 128
E = 8
B = 8
W = 128
VMEM = pl.BlockSpec(memory_space=pltpu.VMEM)


def half_sine_terms(count):
    w = 0.125 * (1 + np.cos(np.pi * (np.arange(64) + 0.5) / 64))
    u = np.sqrt(w)
    target = math.sqrt(2) * np.sin(np.pi * u) / u
    return np.polynomial.polynomial.polyfit(w, target, count - 1)


def phase_map():
    rank = W // 2
    nodes = np.cos(np.float32(math.pi) * (np.arange(rank, dtype=np.float32) + np.float32(0.5)) / np.float32(rank))
    rest = np.tile(nodes.astype(np.float64) * 0.5, 2)
    out = np.zeros((4, E, B, B, W), np.float64)
    for piece in range(3):
        part = rest.astype(jnp.bfloat16).astype(np.float64)
        rest = rest - part
        for b in range(B):
            out[piece, :, b, b, :] = part
    out[3, 0, 0, :, rank:] = -0.25
    return out.reshape(4 * E * B, B * W).astype(jnp.bfloat16)


def low_half(shape):
    return lax.broadcasted_iota(jnp.int32, shape, len(shape) - 1) % W < W // 2


def half_turn(x):
    return pltpu.roll(x, W // 2, x.ndim - 1)


def slot_of(order):
    lane = lax.broadcasted_iota(jnp.int32, order.shape, 1)
    return (lane // 8) * 8 + order


def pack_kernel(charges_ref, order_ref, out_ref):
    rows = 64
    half = PARTS // 2

    def body(step, _):
        at = pl.ds(pl.multiple_of(step * rows, rows), rows)
        index = slot_of(order_ref[at])
        first = jnp.take_along_axis(charges_ref[0, at], index, axis=1, mode="promise_in_bounds")
        second = jnp.take_along_axis(charges_ref[1, at], index, axis=1, mode="promise_in_bounds")
        low = low_half(first.shape)
        even = jnp.where(low, first, half_turn(second)).astype(jnp.bfloat16)
        odd = jnp.where(low, half_turn(first), second).astype(jnp.bfloat16)
        out_ref[pl.ds(step * (rows // E), rows // E)] = even.reshape(rows // E, E, W)
        out_ref[pl.ds(half + step * (rows // E), rows // E)] = odd.reshape(rows // E, E, W)
        return 0

    lax.fori_loop(0, half * E // rows, body, 0)


def unpack_kernel(field_ref, order_ref, out_ref):
    rows = 64
    half = PARTS // 2

    def body(step, _):
        at = pl.ds(pl.multiple_of(step * rows, rows), rows)
        index = slot_of(order_ref[at])
        even = field_ref[pl.ds(step * (rows // E), rows // E)].astype(jnp.float32).reshape(rows, W)
        odd = field_ref[pl.ds(half + step * (rows // E), rows // E)].astype(jnp.float32).reshape(rows, W)
        low = low_half(even.shape)
        first = jnp.where(low, even, half_turn(odd))
        second = jnp.where(low, half_turn(even), odd)
        out_ref[0, at] = jnp.take_along_axis(first, index, axis=1, mode="promise_in_bounds")
        out_ref[1, at] = jnp.take_along_axis(second, index, axis=1, mode="promise_in_bounds")
        return 0

    lax.fori_loop(0, half * E // rows, body, 0)


def place(index, narrow):
    return (index // narrow, index % narrow)


def exchange_kernel(narrow, count, *refs):
    sources, targets, sends, recvs = (refs[i * count : (i + 1) * count] for i in range(4))
    me = lax.axis_index("wide") * narrow + lax.axis_index("narrow")
    barrier = pltpu.get_barrier_semaphore()

    def greet(k, _):
        pl.semaphore_signal(barrier, inc=1, device_id=place(me ^ k, narrow), device_id_type=MESH)
        return 0

    lax.fori_loop(1, PARTS, greet, 0)
    pl.semaphore_wait(barrier, PARTS - 1)

    def send(k, _):
        to = me ^ k
        for i in reversed(range(count)):
            pltpu.make_async_remote_copy(
                sources[i].at[to], targets[i].at[me], sends[i], recvs[i],
                device_id=place(to, narrow), device_id_type=MESH,
            ).start()
        return 0

    lax.fori_loop(1, PARTS, send, 0)
    for i in range(count):
        targets[i][me] = sources[i][me]
    others = pl.ds(0, PARTS - 1)
    for i in range(count):
        for sem in (recvs[i], sends[i]):
            pltpu.make_async_copy(sources[i].at[others], targets[i].at[others], sem).wait()


def exchange(narrow, arrays, collective_id):
    count = len(arrays)
    return pl.pallas_call(
        functools.partial(exchange_kernel, narrow, count),
        out_shape=tuple(jax.ShapeDtypeStruct(a.shape, a.dtype) for a in arrays),
        in_specs=[VMEM] * count,
        out_specs=(VMEM,) * count,
        scratch_shapes=[pltpu.SemaphoreType.DMA] * (2 * count),
        compiler_params=pltpu.CompilerParams(has_side_effects=True, collective_id=collective_id),
    )(*arrays)


def rotate(pre, turn):
    low = low_half(turn.shape)
    other = half_turn(turn)
    cosine = jnp.where(low, turn, other)
    sine = jnp.where(low, -other, turn)
    return pre * cosine + half_turn(pre) * sine


def level_map(mixing_ref, level):
    return jnp.concatenate(
        [jnp.concatenate([mixing_ref[level, j, i] for i in range(2)], axis=0) for j in range(2)], axis=1
    )


def pair_up(even, odd):
    rows = even.shape[0]
    both = jnp.concatenate([even.reshape(rows // E, E, W), odd.reshape(rows // E, E, W)], axis=1)
    return both.reshape(2 * rows, W)


def levels_kernel(
    leaf_ref, speed_ref, leaf_map_ref, mixing_ref, eval_map_ref, phase_ref, out_ref, state, turn_p, turn_q
):
    terms = half_sine_terms(5)
    early = {0: 0, 1: 1, 9: 2}

    nd = 8

    def turns(step, _):
        rows = nd * E
        at = pl.ds(pl.multiple_of(step * nd, nd), nd)
        speeds = jnp.broadcast_to(speed_ref[at].astype(jnp.float32), (nd, E, W)).reshape(rows, W)
        lane = lax.broadcasted_iota(jnp.int32, (rows, W), 1)
        row = lax.broadcasted_iota(jnp.int32, (rows, W), 0)
        own = jnp.where((lane % 64) // B == row % E, speeds, 0.0)
        tail = jnp.where(lane < 64, own, jnp.where(lane == 64, 1.0, 0.0))
        operand = jnp.concatenate([own, tail], axis=1).astype(jnp.bfloat16)
        turn_count = jnp.dot(operand, phase_ref[...], preferred_element_type=jnp.float32)
        low = low_half((rows, W))
        rows_at = pl.ds(pl.multiple_of(step * rows, rows), rows)
        wide_at = pl.ds(pl.multiple_of(step * rows * 2, rows * 2), rows * 2)
        for pair in range(B // 2):
            now, before, twice = [], [], []
            for b in (2 * pair, 2 * pair + 1):
                u = turn_count[:, b * W : (b + 1) * W]
                u = u - jnp.round(u)
                w = u * u
                p = jnp.float32(terms[4])
                for k in (3, 2, 1, 0):
                    p = p * w + jnp.float32(terms[k])
                s = u * p
                t = 1.0 - s * s
                now.append(t)
                before.append(jnp.where(low, 1.0, 0.0))
                c = jnp.where(low, t, half_turn(t))
                twice.append(c + c)
            for level in range(LEVELS):
                if level in early:
                    for i in range(2):
                        turn_p[early[level], 2 * pair + i, rows_at] = now[i].astype(jnp.bfloat16)
                else:
                    turn_q[level - 2, pair, wide_at] = pair_up(now[0], now[1]).astype(jnp.bfloat16)
                if level < LEVELS - 1:
                    now, before = [twice[i] * now[i] - before[i] for i in range(2)], now
        return 0

    lax.fori_loop(0, PARTS // nd, turns, 0)

    nl = 16

    def first_levels(step, _):
        rows = nl * E
        at = pl.ds(pl.multiple_of(step * nl, nl), nl)
        rows_at = pl.ds(pl.multiple_of(step * rows, rows), rows)
        wide_at = pl.ds(pl.multiple_of(step * rows * 2, rows * 2), rows * 2)
        leaf = leaf_ref[at].reshape(rows, W)
        spread = jnp.dot(leaf, leaf_map_ref[...], preferred_element_type=jnp.float32).astype(jnp.bfloat16)
        boxes = [spread[:, b * W : (b + 1) * W] for b in range(B)]
        for level in range(3):
            maps = level_map(mixing_ref, level)
            pres = [None] * B
            for b in range(B):
                if b >> level & 1:
                    continue
                far = b | 1 << level
                pre = jnp.dot(
                    jnp.concatenate([boxes[b], boxes[far]], axis=1), maps, preferred_element_type=jnp.float32
                )
                pres[b], pres[far] = pre[:, :W], pre[:, W:]
            if level < 2:
                boxes = [
                    rotate(pres[b].astype(jnp.bfloat16), turn_p[early[level], b, rows_at]) for b in range(B)
                ]
            else:
                for pair in range(B // 2):
                    pre = pair_up(pres[2 * pair], pres[2 * pair + 1]).astype(jnp.bfloat16)
                    state[pair, wide_at] = rotate(pre, turn_q[0, pair, wide_at])
        return 0

    lax.fori_loop(0, PARTS // nl, first_levels, 0)

    for level in range(3, LEVELS - 1):
        stride = 2 * E << (level - 3)
        block = min(stride, 512)
        per = stride // block
        group = 512 // block
        maps = level_map(mixing_ref, level)
        steps_of_pair = PARTS * 2 * E // (2 * block * group)

        def later(step, _, level=level, stride=stride, block=block, per=per, group=group, maps=maps):
            pair = step // steps_of_pair
            inner = step % steps_of_pair
            near, far = [], []
            for g in range(group):
                unit = inner * group + g
                start = (unit // per) * (2 * stride) + (unit % per) * block
                near.append(pl.ds(pl.multiple_of(start, block), block))
                far.append(pl.ds(pl.multiple_of(start + stride, block), block))
            lhs = jnp.concatenate(
                [
                    jnp.concatenate([state[pair, at] for at in near], axis=0),
                    jnp.concatenate([state[pair, at] for at in far], axis=0),
                ],
                axis=1,
            )
            pre = jnp.dot(lhs, maps, preferred_element_type=jnp.float32)
            for g in range(group):
                for side, at in ((0, near[g]), (1, far[g])):
                    own = pre[g * block : (g + 1) * block, side * W : (side + 1) * W].astype(jnp.bfloat16)
                    state[pair, at] = rotate(own, turn_q[level - 2, pair, at])
            return 0

        lax.fori_loop(0, (B // 2) * steps_of_pair, later, 0)

    last = LEVELS - 1
    ne = 16

    def finish(step, _):
        rows = ne * 2 * E
        maps = level_map(mixing_ref, last)
        half = PARTS * E // 2
        near = pl.ds(pl.multiple_of(step * rows, rows), rows)
        far = pl.ds(pl.multiple_of(step * rows + 2 * half, rows), rows)
        boxes = [[None] * B for _ in range(2)]
        for pair in range(B // 2):
            lhs = jnp.concatenate([state[pair, near], state[pair, far]], axis=1)
            pre = jnp.dot(lhs, maps, preferred_element_type=jnp.float32)
            for side in range(2):
                own = pre[:, side * W : (side + 1) * W].reshape(ne, 2, E, W)
                rows_at = pl.ds(pl.multiple_of(step * ne * E + side * half, ne * E), ne * E)
                for i in range(2):
                    box = own[:, i].reshape(ne * E, W).astype(jnp.bfloat16)
                    boxes[side][2 * pair + i] = rotate(box, turn_p[early[last], 2 * pair + i, rows_at])
        for side in range(2):
            values = jnp.dot(
                jnp.concatenate(boxes[side], axis=1), eval_map_ref[...], preferred_element_type=jnp.float32
            )
            at = pl.ds(step * ne + side * (PARTS // 2), ne)
            out_ref[at] = values.astype(jnp.bfloat16).reshape(ne, E, W)
        return 0

    lax.fori_loop(0, PARTS // 2 // ne, finish, 0)


def on_device(narrow, charges, source_order, velocity, leaf_weight, mixing, eval_weight, target_order):
    lines = charges.shape[1] // W
    eye = jnp.eye(B, dtype=jnp.bfloat16)
    leaf_map = leaf_weight.reshape(2, 1, 8, 1, W) * eye.reshape(1, B, 1, B, 1)
    leaf_map = leaf_map.reshape(W, B * W)
    eval_map = eval_weight.reshape(1, W, 2, 1, 8) * eye.reshape(B, 1, 1, B, 1)
    eval_map = eval_map.reshape(B * W, W)
    half = PARTS // 2
    speeds = velocity.reshape(half, E, 2, B).transpose(2, 0, 1, 3).reshape(PARTS, 1, E * B)
    speeds = jnp.concatenate([speeds, speeds], axis=2)

    packed = pl.pallas_call(
        pack_kernel,
        out_shape=jax.ShapeDtypeStruct((PARTS, E, W), jnp.bfloat16),
        in_specs=[VMEM] * 2,
        out_specs=VMEM,
    )(charges.reshape(2, lines, W), source_order.reshape(lines, W))
    leaf, speeds = exchange(narrow, (packed, speeds), 0)
    values = pl.pallas_call(
        levels_kernel,
        out_shape=jax.ShapeDtypeStruct((PARTS, E, W), jnp.bfloat16),
        in_specs=[VMEM] * 6,
        out_specs=VMEM,
        scratch_shapes=[
            pltpu.VMEM((B // 2, PARTS * 2 * E, W), jnp.bfloat16),
            pltpu.VMEM((3, B, PARTS * E, W), jnp.bfloat16),
            pltpu.VMEM((LEVELS - 3, B // 2, PARTS * 2 * E, W), jnp.bfloat16),
        ],
        compiler_params=pltpu.CompilerParams(vmem_limit_bytes=56 * 2**20),
    )(leaf, speeds, leaf_map, mixing, eval_map, jnp.asarray(phase_map()))
    (field,) = exchange(narrow, (values,), 1)
    out = pl.pallas_call(
        unpack_kernel,
        out_shape=jax.ShapeDtypeStruct((2, lines, W), jnp.float32),
        in_specs=[VMEM] * 2,
        out_specs=VMEM,
    )(field, target_order.reshape(lines, W))
    return out.reshape(2, lines * W)


def solution(mesh):
    both = ("wide", "narrow")
    return jax.shard_map(
        functools.partial(on_device, mesh.shape["narrow"]),
        mesh=mesh,
        in_specs=(P(None, both), P(both), P(both), P(), P(), P(), P(both)),
        out_specs=P(None, both),
        check_vma=False,
    )
```

```python
import functools
import math

import jax
import jax.numpy as jnp
import numpy as np
from jax import lax
from jax.experimental import pallas as pl
from jax.experimental.pallas import tpu as pltpu
from jax.sharding import PartitionSpec as P

MESH = pl.DeviceIdType.MESH
LEVELS = 10
PARTS = 128
E = 8
B = 8
W = 128


def half_sine_terms(count):
    w = 0.125 * (1 + np.cos(np.pi * (np.arange(64) + 0.5) / 64))
    u = np.sqrt(w)
    target = math.sqrt(2) * np.sin(np.pi * u) / u
    return np.polynomial.polynomial.polyfit(w, target, count - 1)


def phase_map():
    rank = W // 2
    nodes = np.cos(np.float32(math.pi) * (np.arange(rank, dtype=np.float32) + np.float32(0.5)) / np.float32(rank))
    rest = np.tile(nodes.astype(np.float64) * 0.5, 2)
    pieces = []
    for _ in range(3):
        pieces.append(rest.astype(jnp.bfloat16).astype(np.float64))
        rest = rest - pieces[-1]
    out = np.zeros((2, E, 2, B, B, W), np.float64)
    for b in range(B):
        out[0, :, 0, b, b, :] = pieces[0]
        out[0, :, 1, b, b, :] = pieces[1]
        out[1, :, :, b, b, :] = pieces[2]
    return out.reshape(2 * W, B * W).astype(jnp.bfloat16)


def low_half(shape):
    return lax.broadcasted_iota(jnp.int32, shape, len(shape) - 1) % W < W // 2


def half_turn(x):
    return pltpu.roll(x, W // 2, x.ndim - 1)


def slot_of(order):
    lane = lax.broadcasted_iota(jnp.int32, order.shape, 1)
    return (lane // 8) * 8 + order


def pack_rows(charges_ref, order_ref, out_ref):
    rows = 64
    half = PARTS // 2

    def body(step, _):
        at = pl.ds(pl.multiple_of(step * rows, rows), rows)
        index = slot_of(order_ref[at])
        first = charges_ref[pl.ds(pl.multiple_of(step * 2 * rows, 2 * rows), rows, stride=2)]
        second = charges_ref[pl.ds(step * 2 * rows + 1, rows, stride=2)]
        first = jnp.take_along_axis(first, index, axis=1, mode="promise_in_bounds")
        second = jnp.take_along_axis(second, index, axis=1, mode="promise_in_bounds")
        low = low_half(first.shape)
        even = jnp.where(low, first, half_turn(second)).astype(jnp.bfloat16)
        odd = jnp.where(low, half_turn(first), second).astype(jnp.bfloat16)
        out_ref[pl.ds(step * (rows // E), rows // E)] = even.reshape(rows // E, E, W)
        out_ref[pl.ds(half + step * (rows // E), rows // E)] = odd.reshape(rows // E, E, W)
        return 0

    lax.fori_loop(0, half * E // rows, body, 0)


def unpack_rows(field_ref, order_ref, out_ref):
    rows = 64
    half = PARTS // 2

    def body(step, _):
        at = pl.ds(pl.multiple_of(step * rows, rows), rows)
        index = slot_of(order_ref[at])
        even = field_ref[pl.ds(step * (rows // E), rows // E)].astype(jnp.float32).reshape(rows, W)
        odd = field_ref[pl.ds(half + step * (rows // E), rows // E)].astype(jnp.float32).reshape(rows, W)
        low = low_half(even.shape)
        first = jnp.where(low, even, half_turn(odd))
        second = jnp.where(low, half_turn(even), odd)
        first = jnp.take_along_axis(first, index, axis=1, mode="promise_in_bounds")
        second = jnp.take_along_axis(second, index, axis=1, mode="promise_in_bounds")
        out_ref[pl.ds(pl.multiple_of(step * 2 * rows, 2 * rows), rows, stride=2)] = first
        out_ref[pl.ds(step * 2 * rows + 1, rows, stride=2)] = second
        return 0

    lax.fori_loop(0, half * E // rows, body, 0)


def place(index, narrow):
    return (index // narrow, index % narrow)


def build_maps(leaf_ref, eval_ref, leaf_map_ref, eval_map_ref):
    leaf_map_ref[...] = jnp.zeros(leaf_map_ref.shape, jnp.bfloat16)
    for c in range(2):
        for b in range(B):
            rows = pl.ds(c * 64 + b * 8, 8)
            leaf_map_ref[rows, pl.ds(b * W, W)] = leaf_ref[pl.ds(c * 8, 8)]
    row = lax.broadcasted_iota(jnp.int32, (16, W), 0)
    lane = lax.broadcasted_iota(jnp.int32, (16, W), 1)
    slot = (lane // 64) * 8 + lane % 8 == row
    for b in range(B):
        pick = jnp.where(slot & (lane % 64 // 8 == b), 1.0, 0.0).astype(jnp.bfloat16)
        block = lax.dot_general(
            eval_ref[...], pick, (((0,), (0,)), ((), ())), preferred_element_type=jnp.float32
        )
        eval_map_ref[pl.ds(b * W, W)] = block.astype(jnp.bfloat16)


def rotate(pre, turn):
    low = low_half(turn.shape)
    other = half_turn(turn)
    cosine = jnp.where(low, turn, other)
    sine = jnp.where(low, -other, turn)
    return pre * cosine + half_turn(pre) * sine


def level_map(mixing_ref, level):
    return jnp.concatenate(
        [jnp.concatenate([mixing_ref[level, j, i] for i in range(2)], axis=0) for j in range(2)], axis=1
    )


def mix(near, far, maps):
    pre = jnp.dot(jnp.concatenate([near, far], axis=1), maps, preferred_element_type=jnp.float32)
    return [pre[:, :W], pre[:, W:]]


def pair_up(even, odd):
    rows = even.shape[0]
    both = jnp.concatenate([even.reshape(rows // E, E, W), odd.reshape(rows // E, E, W)], axis=1)
    return both.reshape(2 * rows, W)


TURN_ND, FIRST_ND, LATER_PAIRS, LAST_ND = 8, 32, 2, 16
PAIRS = B // 2
ROWS = PARTS * E
EARLY = {0: 0, 1: 1, LEVELS - 1: 2}


def make_turns(own_half, speed_ref, phase_ref, turn_p, turn_q):
    terms = half_sine_terms(5)
    nd = TURN_ND
    rows = nd * E

    def body(step, _):
        at = pl.ds(pl.multiple_of(step * nd, nd), nd)
        speeds = jnp.broadcast_to(speed_ref[at], (nd, E, W)).reshape(rows, W)
        lane = lax.broadcasted_iota(jnp.int32, (rows, W), 1)
        row = lax.broadcasted_iota(jnp.int32, (rows, W), 0)
        mine = (lane // 16 == row % E) & (lane // B % 2 == own_half)
        own = jnp.where(mine, speeds, 0.0)
        operand = jnp.concatenate([own + pltpu.roll(own, B, 1), own], axis=1).astype(jnp.bfloat16)
        counts = jnp.dot(operand, phase_ref[...], preferred_element_type=jnp.float32)
        low = low_half((rows, W))
        start = jnp.where(low, 1.0, 0.0)
        quarter = jnp.where(low, 0.0, 0.25)
        rows_at = pl.ds(pl.multiple_of(step * rows, rows), rows)
        wide_at = pl.ds(pl.multiple_of(step * rows * 2, rows * 2), rows * 2)
        for pair in range(PAIRS):
            now, before, twice = [], [start, start], []
            for b in (2 * pair, 2 * pair + 1):
                u = counts[:, b * W : (b + 1) * W] - quarter
                u = u - jnp.round(u)
                w = u * u
                p = w * jnp.float32(terms[4]) + jnp.float32(terms[3])
                for k in (2, 1, 0):
                    p = p * w + jnp.float32(terms[k])
                s = u * p
                t = 1.0 - s * s
                now.append(t)
                c = jnp.where(low, t, half_turn(t))
                twice.append(c + c)
            for level in range(LEVELS):
                if level in EARLY:
                    for i in range(2):
                        turn_p[EARLY[level], 2 * pair + i, rows_at] = now[i].astype(jnp.bfloat16)
                else:
                    turn_q[level - 2, pair, wide_at] = pair_up(now[0], now[1]).astype(jnp.bfloat16)
                if level < LEVELS - 1:
                    now, before = [twice[i] * now[i] - before[i] for i in range(2)], now
        return 0

    lax.fori_loop(0, PARTS // nd, body, 0)


def first_levels(leaf_ref, leaf_map_ref, mixing_ref, turn_p, turn_q, state):
    nd = FIRST_ND
    rows = nd * E

    def body(step, _):
        at = pl.ds(pl.multiple_of(step * nd, nd), nd)
        rows_at = pl.ds(pl.multiple_of(step * rows, rows), rows)
        wide_at = pl.ds(pl.multiple_of(step * rows * 2, rows * 2), rows * 2)
        leaf = leaf_ref[at].reshape(rows, W)
        boxes = [None] * B
        maps = level_map(mixing_ref, 0)
        for pair in range(PAIRS):
            lanes = pl.ds(pair * 2 * W, 2 * W)
            spread = jnp.dot(leaf, leaf_map_ref[:, lanes], preferred_element_type=jnp.float32)
            pre = jnp.dot(spread.astype(jnp.bfloat16), maps, preferred_element_type=jnp.float32)
            for i in range(2):
                b = 2 * pair + i
                boxes[b] = rotate(pre[:, i * W : (i + 1) * W].astype(jnp.bfloat16), turn_p[0, b, rows_at])
        maps = level_map(mixing_ref, 1)
        for b in (0, 1, 4, 5):
            for i, pre in enumerate(mix(boxes[b], boxes[b + 2], maps)):
                boxes[b + 2 * i] = rotate(pre.astype(jnp.bfloat16), turn_p[1, b + 2 * i, rows_at])
        maps = level_map(mixing_ref, 2)
        for pair in range(2):
            pres = [mix(boxes[2 * pair + i], boxes[2 * pair + i + 4], maps) for i in range(2)]
            for i in range(2):
                pre = pair_up(pres[0][i], pres[1][i]).astype(jnp.bfloat16)
                state[pair + 2 * i, wide_at] = rotate(pre, turn_q[0, pair + 2 * i, wide_at])
        return 0

    lax.fori_loop(0, PARTS // nd, body, 0)


def later_level(level, mixing_ref, turn_q, source, target):
    stride = 2 * E << (level - 3)
    starts = range(0, 2 * ROWS, 2 * stride)

    def body(step, _):
        maps = level_map(mixing_ref, level)
        for i in range(LATER_PAIRS):
            pair = step * LATER_PAIRS + i
            near = jnp.concatenate([source[pair, pl.ds(at, stride)] for at in starts], axis=0)
            far = jnp.concatenate([source[pair, pl.ds(at + stride, stride)] for at in starts], axis=0)
            for side, pre in enumerate(mix(near, far, maps)):
                for n, at in enumerate(starts):
                    rows_at = pl.ds(at + side * stride, stride)
                    part = pre[n * stride : (n + 1) * stride].astype(jnp.bfloat16)
                    target[pair, rows_at] = rotate(part, turn_q[level - 2, pair, rows_at])
        return 0

    lax.fori_loop(0, PAIRS // LATER_PAIRS, body, 0)


def last_level(me, send, mixing_ref, eval_map_ref, turn_p, state, out_ref):
    level = LEVELS - 1
    nd = LAST_ND
    rows = nd * E
    steps = PARTS // 2 // nd

    def body(count, _):
        step = (count + me // nd) % steps
        maps = level_map(mixing_ref, level)
        boxes = [[], []]
        wide = [pl.ds(pl.multiple_of(step * 2 * rows + side * ROWS, 2 * rows), 2 * rows) for side in range(2)]
        for pair in range(PAIRS):
            for side, pre in enumerate(mix(state[pair, wide[0]], state[pair, wide[1]], maps)):
                own = pre.reshape(nd, 2, E, W)
                rows_at = pl.ds(pl.multiple_of(step * rows + side * (ROWS // 2), rows), rows)
                for i in range(2):
                    box = own[:, i].reshape(rows, W).astype(jnp.bfloat16)
                    boxes[side].append(rotate(box, turn_p[EARLY[level], 2 * pair + i, rows_at]))
        for side in range(2):
            values = jnp.dot(
                jnp.concatenate(boxes[side], axis=1), eval_map_ref[...], preferred_element_type=jnp.float32
            )
            at = pl.ds(step * nd + side * (PARTS // 2), nd)
            out_ref[at] = values.astype(jnp.bfloat16).reshape(nd, E, W)

        def one(i, _):
            for side in range(2):
                send(step * nd + side * (PARTS // 2) + ((i + me) % nd))
            return 0

        lax.fori_loop(0, nd, one, 0)
        return 0

    lax.fori_loop(0, steps, body, 0)


def kernel(
    narrow, charges_hbm, order_hbm, speed_hbm, leaf_hbm, mixing_hbm, eval_hbm, target_hbm, phase_hbm, out_hbm,
    charges, order, speed, leaf_weight, mixing, eval_weight, target, phase,
    speed_rows, speeds, packed, leaf, result, field, out, leaf_map, eval_map, state, spare, turn_p, turn_q,
    load_sems, sends, recvs, store_sem,
):
    me = lax.axis_index("wide") * narrow + lax.axis_index("narrow")
    barrier = pltpu.get_barrier_semaphore()

    def greet(k, _):
        pl.semaphore_signal(barrier, inc=1, device_id=place(me ^ k, narrow), device_id_type=MESH)
        return 0

    lax.fori_loop(1, PARTS, greet, 0)
    pairs = (
        (speed_hbm, speed), (order_hbm, order), (charges_hbm, charges), (leaf_hbm, leaf_weight),
        (eval_hbm, eval_weight), (phase_hbm, phase), (mixing_hbm, mixing), (target_hbm, target),
    )
    loads = [pltpu.make_async_copy(a, b, load_sems.at[i]) for i, (a, b) in enumerate(pairs)]
    for load in loads:
        load.start()
    half = PARTS // 2
    loads[0].wait()
    speed_rows[...] = speed[...].astype(jnp.float32).reshape(half, 1, W)
    loads[1].wait()
    loads[2].wait()
    pack_rows(charges, order, packed)
    loads[3].wait()
    loads[4].wait()
    build_maps(leaf_weight, eval_weight, leaf_map, eval_map)
    pl.semaphore_wait(barrier, PARTS - 1)

    def remote(source, target, i, to):
        return pltpu.make_async_remote_copy(
            source, target.at[me], sends.at[i], recvs.at[i], device_id=place(to, narrow), device_id_type=MESH
        )

    def send_speed(k, _):
        to = me ^ k
        remote(speed_rows.at[to % half], speeds, 0, to).start()
        return 0

    def send_leaf(k, _):
        to = me ^ k
        remote(packed.at[to], leaf, 1, to).start()
        return 0

    lax.fori_loop(1, PARTS, send_speed, 0)
    lax.fori_loop(1, PARTS, send_leaf, 0)
    speeds[me] = speed_rows[me % half]
    leaf[me] = packed[me]
    others = pl.ds(0, PARTS - 1)

    def wait(ref, sem):
        pltpu.make_async_copy(ref.at[others], ref.at[others], sem).wait()

    loads[5].wait()
    wait(speeds, recvs.at[0])
    make_turns(me // half, speeds, phase, turn_p, turn_q)
    loads[6].wait()
    wait(leaf, recvs.at[1])
    first_levels(leaf, leaf_map, mixing, turn_p, turn_q, state)
    now, later = state, spare
    for level in range(3, LEVELS - 1):
        later_level(level, mixing, turn_q, now, later)
        now, later = later, now

    def send_result(to):
        @pl.when(to != me)
        def _():
            remote(result.at[to], field, 2, to).start()

    last_level(me, send_result, mixing, eval_map, turn_p, now, result)
    field[me] = result[me]
    loads[7].wait()
    wait(field, recvs.at[2])
    unpack_rows(field, target, out)
    store = pltpu.make_async_copy(out, out_hbm, store_sem)
    store.start()
    wait(speeds, sends.at[0])
    wait(packed, sends.at[1])
    wait(result, sends.at[2])
    store.wait()


def on_device(narrow, charges, source_order, velocity, leaf_weight, mixing, eval_weight, target_order):
    lines = charges.shape[1] // W
    half = PARTS // 2
    args = (
        charges.reshape(2, lines, W).transpose(1, 0, 2).reshape(2 * lines, W),
        source_order.reshape(lines, W),
        velocity.reshape(half, W),
        leaf_weight,
        mixing,
        eval_weight.T,
        target_order.reshape(lines, W),
        jnp.asarray(phase_map()),
    )
    chunk = pltpu.VMEM((PARTS, E, W), jnp.bfloat16)
    states = pltpu.VMEM((PAIRS, 2 * ROWS, W), jnp.bfloat16)
    rows = pltpu.VMEM((2 * lines, W), jnp.float32)
    out = pl.pallas_call(
        functools.partial(kernel, narrow),
        out_shape=jax.ShapeDtypeStruct((2 * lines, W), jnp.float32),
        in_specs=[pl.BlockSpec(memory_space=pltpu.HBM)] * len(args),
        out_specs=pl.BlockSpec(memory_space=pltpu.HBM),
        scratch_shapes=[pltpu.VMEM(a.shape, a.dtype) for a in args]
        + [
            pltpu.VMEM((half, 1, W), jnp.float32),
            pltpu.VMEM((PARTS, 1, W), jnp.float32),
            chunk,
            chunk,
            chunk,
            chunk,
            rows,
            pltpu.VMEM((W, B * W), jnp.bfloat16),
            pltpu.VMEM((B * W, W), jnp.bfloat16),
            states,
            states,
            pltpu.VMEM((len(EARLY), B, ROWS, W), jnp.bfloat16),
            pltpu.VMEM((LEVELS - len(EARLY), PAIRS, 2 * ROWS, W), jnp.bfloat16),
            pltpu.SemaphoreType.DMA((len(args),)),
            pltpu.SemaphoreType.DMA((3,)),
            pltpu.SemaphoreType.DMA((3,)),
            pltpu.SemaphoreType.DMA,
        ],
        compiler_params=pltpu.CompilerParams(
            has_side_effects=True, collective_id=0, vmem_limit_bytes=62 * 2**20
        ),
    )(*args)
    return out.reshape(lines, 2, W).transpose(1, 0, 2).reshape(2, lines * W)


def solution(mesh):
    both = ("wide", "narrow")
    return jax.shard_map(
        functools.partial(on_device, mesh.shape["narrow"]),
        mesh=mesh,
        in_specs=(P(None, both), P(both), P(both), P(), P(), P(), P(both)),
        out_specs=P(None, both),
        check_vma=False,
    )
```

```python
import functools
import math

import jax
import jax.numpy as jnp
import numpy as np
from jax import lax
from jax.experimental import pallas as pl
from jax.experimental.pallas import tpu as pltpu
from jax.sharding import PartitionSpec as P

MESH = pl.DeviceIdType.MESH
LEVELS = 10
PARTS = 128
E = 8
B = 8
W = 128


def half_sine_terms(count):
    w = 0.125 * (1 + np.cos(np.pi * (np.arange(64) + 0.5) / 64))
    u = np.sqrt(w)
    target = math.sqrt(2) * np.sin(np.pi * u) / u
    return np.polynomial.polynomial.polyfit(w, target, count - 1)


def phase_map():
    rank = W // 2
    nodes = np.cos(np.float32(math.pi) * (np.arange(rank, dtype=np.float32) + np.float32(0.5)) / np.float32(rank))
    rest = np.tile(nodes.astype(np.float64) * 0.5, 2)
    pieces = []
    for _ in range(3):
        pieces.append(rest.astype(jnp.bfloat16).astype(np.float64))
        rest = rest - pieces[-1]
    out = np.zeros((2, E, 2, B, B, W), np.float64)
    for b in range(B):
        out[0, :, 0, b, b, :] = pieces[0]
        out[0, :, 1, b, b, :] = pieces[1]
        out[1, :, :, b, b, :] = pieces[2]
    return out.reshape(2 * W, B * W).astype(jnp.bfloat16)


def low_half(shape):
    return lax.broadcasted_iota(jnp.int32, shape, len(shape) - 1) % W < W // 2


def half_turn(x):
    return pltpu.roll(x, W // 2, x.ndim - 1)


def slot_of(order):
    lane = lax.broadcasted_iota(jnp.int32, order.shape, 1)
    return (lane // 8) * 8 + order


def pack_rows(charges_ref, order_ref, out_ref):
    rows = 64
    half = PARTS // 2

    def body(step, _):
        at = pl.ds(pl.multiple_of(step * rows, rows), rows)
        index = slot_of(order_ref[at])
        first = charges_ref[pl.ds(pl.multiple_of(step * 2 * rows, 2 * rows), rows, stride=2)]
        second = charges_ref[pl.ds(step * 2 * rows + 1, rows, stride=2)]
        first = jnp.take_along_axis(first, index, axis=1, mode="promise_in_bounds")
        second = jnp.take_along_axis(second, index, axis=1, mode="promise_in_bounds")
        low = low_half(first.shape)
        even = jnp.where(low, first, half_turn(second)).astype(jnp.bfloat16)
        odd = jnp.where(low, half_turn(first), second).astype(jnp.bfloat16)
        out_ref[pl.ds(step * (rows // E), rows // E)] = even.reshape(rows // E, E, W)
        out_ref[pl.ds(half + step * (rows // E), rows // E)] = odd.reshape(rows // E, E, W)
        return 0

    lax.fori_loop(0, half * E // rows, body, 0)


def unpack_rows(field_ref, order_ref, out_ref):
    rows = 64
    half = PARTS // 2

    def body(step, _):
        at = pl.ds(pl.multiple_of(step * rows, rows), rows)
        index = slot_of(order_ref[at])
        even = field_ref[pl.ds(step * (rows // E), rows // E)].astype(jnp.float32).reshape(rows, W)
        odd = field_ref[pl.ds(half + step * (rows // E), rows // E)].astype(jnp.float32).reshape(rows, W)
        low = low_half(even.shape)
        first = jnp.where(low, even, half_turn(odd))
        second = jnp.where(low, half_turn(even), odd)
        first = jnp.take_along_axis(first, index, axis=1, mode="promise_in_bounds")
        second = jnp.take_along_axis(second, index, axis=1, mode="promise_in_bounds")
        out_ref[pl.ds(pl.multiple_of(step * 2 * rows, 2 * rows), rows, stride=2)] = first
        out_ref[pl.ds(step * 2 * rows + 1, rows, stride=2)] = second
        return 0

    lax.fori_loop(0, half * E // rows, body, 0)


def place(index, narrow):
    return (index // narrow, index % narrow)


def build_maps(leaf_ref, eval_ref, leaf_map_ref, eval_map_ref):
    leaf_map_ref[...] = jnp.zeros(leaf_map_ref.shape, jnp.bfloat16)
    for c in range(2):
        for b in range(B):
            rows = pl.ds(c * 64 + b * 8, 8)
            leaf_map_ref[rows, pl.ds(b * W, W)] = leaf_ref[pl.ds(c * 8, 8)]
    row = lax.broadcasted_iota(jnp.int32, (16, W), 0)
    lane = lax.broadcasted_iota(jnp.int32, (16, W), 1)
    slot = (lane // 64) * 8 + lane % 8 == row
    for b in range(B):
        pick = jnp.where(slot & (lane % 64 // 8 == b), 1.0, 0.0).astype(jnp.bfloat16)
        block = lax.dot_general(
            eval_ref[...], pick, (((0,), (0,)), ((), ())), preferred_element_type=jnp.float32
        )
        eval_map_ref[pl.ds(b * W, W)] = block.astype(jnp.bfloat16)


def rotate(pre, cosine, sine):
    return pre * cosine + half_turn(pre) * sine


def level_map(mixing_ref, level):
    return jnp.concatenate(
        [jnp.concatenate([mixing_ref[level, j, i] for i in range(2)], axis=0) for j in range(2)], axis=1
    )


def mix(near, far, maps):
    pre = jnp.dot(jnp.concatenate([near, far], axis=1), maps, preferred_element_type=jnp.float32)
    return [pre[:, :W], pre[:, W:]]


def pair_up(even, odd):
    rows = even.shape[0]
    both = jnp.concatenate([even.reshape(rows // E, E, W), odd.reshape(rows // E, E, W)], axis=1)
    return both.reshape(2 * rows, W)


TURN_ND, FIRST_ND, LATER_PAIRS, LAST_ND = 8, 64, 2, 16
PAIRS = B // 2
ROWS = PARTS * E
EARLY = {0: 0, 1: 1, LEVELS - 1: 2}


def make_turns(own_half, speed_ref, phase_ref, cos_p, sin_p, cos_q, sin_q):
    terms = half_sine_terms(4)
    nd = TURN_ND
    rows = nd * E

    def body(step, _):
        at = pl.ds(pl.multiple_of(step * nd, nd), nd)
        speeds = jnp.broadcast_to(speed_ref[at], (nd, E, W)).reshape(rows, W)
        lane = lax.broadcasted_iota(jnp.int32, (rows, W), 1)
        row = lax.broadcasted_iota(jnp.int32, (rows, W), 0)
        mine = (lane // 16 == row % E) & (lane // B % 2 == own_half)
        own = jnp.where(mine, speeds, 0.0)
        operand = jnp.concatenate([own + pltpu.roll(own, B, 1), own], axis=1).astype(jnp.bfloat16)
        counts = jnp.dot(operand, phase_ref[...], preferred_element_type=jnp.float32)
        low = low_half((rows, W))
        quarter = jnp.where(low, 0.0, 0.25)
        rows_at = pl.ds(pl.multiple_of(step * rows, rows), rows)
        wide_at = pl.ds(pl.multiple_of(step * rows * 2, rows * 2), rows * 2)
        for pair in range(PAIRS):
            cosine, sine, twice = [], [], []
            for b in (2 * pair, 2 * pair + 1):
                u = counts[:, b * W : (b + 1) * W] - quarter
                u = u - jnp.round(u)
                w = u * u
                p = w * jnp.float32(terms[3]) + jnp.float32(terms[2])
                for k in (1, 0):
                    p = p * w + jnp.float32(terms[k])
                s = u * p
                t = 1.0 - s * s
                other = half_turn(t)
                cosine.append(jnp.where(low, t, other))
                sine.append(jnp.where(low, -other, t))
                twice.append(cosine[-1] + cosine[-1])
            last = None
            for level in range(LEVELS):
                for now, early, late in ((cosine, cos_p, cos_q), (sine, sin_p, sin_q)):
                    if level in EARLY:
                        for i in range(2):
                            early[EARLY[level], 2 * pair + i, rows_at] = now[i].astype(jnp.bfloat16)
                    else:
                        late[level - 2, pair, wide_at] = pair_up(now[0], now[1]).astype(jnp.bfloat16)
                if level == LEVELS - 1:
                    break
                if last is None:
                    after = [twice[i] * cosine[i] - 1.0 for i in range(2)], [twice[i] * sine[i] for i in range(2)]
                else:
                    after = [
                        [twice[i] * now[i] - before[i] for i in range(2)]
                        for now, before in ((cosine, last[0]), (sine, last[1]))
                    ]
                last = cosine, sine
                cosine, sine = after
        return 0

    lax.fori_loop(0, PARTS // nd, body, 0)


def first_levels(leaf_ref, leaf_map_ref, mixing_ref, cos_p, sin_p, cos_q, sin_q, state):
    nd = FIRST_ND
    rows = nd * E

    def body(step, _):
        at = pl.ds(pl.multiple_of(step * nd, nd), nd)
        rows_at = pl.ds(pl.multiple_of(step * rows, rows), rows)
        wide_at = pl.ds(pl.multiple_of(step * rows * 2, rows * 2), rows * 2)
        leaf = leaf_ref[at].reshape(rows, W)
        boxes = [None] * B
        maps = level_map(mixing_ref, 0)
        for pair in range(PAIRS):
            lanes = pl.ds(pair * 2 * W, 2 * W)
            spread = jnp.dot(leaf, leaf_map_ref[:, lanes], preferred_element_type=jnp.float32)
            pre = jnp.dot(spread.astype(jnp.bfloat16), maps, preferred_element_type=jnp.float32)
            for i in range(2):
                b = 2 * pair + i
                boxes[b] = rotate(pre[:, i * W : (i + 1) * W].astype(jnp.bfloat16), cos_p[0, b, rows_at], sin_p[0, b, rows_at])
        maps = level_map(mixing_ref, 1)
        for b in (0, 1, 4, 5):
            for i, pre in enumerate(mix(boxes[b], boxes[b + 2], maps)):
                box = b + 2 * i
                boxes[box] = rotate(pre.astype(jnp.bfloat16), cos_p[1, box, rows_at], sin_p[1, box, rows_at])
        maps = level_map(mixing_ref, 2)
        for pair in range(2):
            pres = [mix(boxes[2 * pair + i], boxes[2 * pair + i + 4], maps) for i in range(2)]
            for i in range(2):
                pre = pair_up(pres[0][i], pres[1][i]).astype(jnp.bfloat16)
                unit = pair + 2 * i
                state[unit, wide_at] = rotate(pre, cos_q[0, unit, wide_at], sin_q[0, unit, wide_at])
        return 0

    lax.fori_loop(0, PARTS // nd, body, 0)


def later_level(level, mixing_ref, cos_q, sin_q, source, target):
    stride = 2 * E << (level - 3)
    starts = range(0, 2 * ROWS, 2 * stride)

    def body(step, _):
        maps = level_map(mixing_ref, level)
        for i in range(LATER_PAIRS):
            pair = step * LATER_PAIRS + i
            near = jnp.concatenate([source[pair, pl.ds(at, stride)] for at in starts], axis=0)
            far = jnp.concatenate([source[pair, pl.ds(at + stride, stride)] for at in starts], axis=0)
            for side, pre in enumerate(mix(near, far, maps)):
                for n, at in enumerate(starts):
                    rows_at = pl.ds(at + side * stride, stride)
                    part = pre[n * stride : (n + 1) * stride].astype(jnp.bfloat16)
                    target[pair, rows_at] = rotate(
                        part, cos_q[level - 2, pair, rows_at], sin_q[level - 2, pair, rows_at]
                    )
        return 0

    lax.fori_loop(0, PAIRS // LATER_PAIRS, body, 0)


def last_level(me, send, mixing_ref, eval_map_ref, cos_p, sin_p, state, out_ref):
    level = LEVELS - 1
    nd = LAST_ND
    rows = nd * E
    steps = PARTS // 2 // nd

    def body(count, _):
        step = (count + me // nd) % steps
        maps = level_map(mixing_ref, level)
        boxes = [[], []]
        wide = [pl.ds(pl.multiple_of(step * 2 * rows + side * ROWS, 2 * rows), 2 * rows) for side in range(2)]
        for pair in range(PAIRS):
            for side, pre in enumerate(mix(state[pair, wide[0]], state[pair, wide[1]], maps)):
                own = pre.reshape(nd, 2, E, W)
                rows_at = pl.ds(pl.multiple_of(step * rows + side * (ROWS // 2), rows), rows)
                for i in range(2):
                    box = own[:, i].reshape(rows, W).astype(jnp.bfloat16)
                    at = EARLY[level], 2 * pair + i, rows_at
                    boxes[side].append(rotate(box, cos_p[at], sin_p[at]))
        for side in range(2):
            values = jnp.dot(
                jnp.concatenate(boxes[side], axis=1), eval_map_ref[...], preferred_element_type=jnp.float32
            )
            at = pl.ds(step * nd + side * (PARTS // 2), nd)
            out_ref[at] = values.astype(jnp.bfloat16).reshape(nd, E, W)

        def one(i, _):
            for side in range(2):
                send(step * nd + side * (PARTS // 2) + ((i + me) % nd))
            return 0

        lax.fori_loop(0, nd, one, 0)
        return 0

    lax.fori_loop(0, steps, body, 0)


def kernel(
    narrow, charges_hbm, order_hbm, speed_hbm, leaf_hbm, mixing_hbm, eval_hbm, target_hbm, phase_hbm, out_hbm,
    charges, order, speed, leaf_weight, mixing, eval_weight, target, phase,
    speed_rows, speeds, packed, leaf, result, field, out, leaf_map, eval_map, state, spare, cos_p, sin_p, cos_q, sin_q,
    load_sems, sends, recvs, store_sem,
):
    me = lax.axis_index("wide") * narrow + lax.axis_index("narrow")
    barrier = pltpu.get_barrier_semaphore()

    def greet(k, _):
        pl.semaphore_signal(barrier, inc=1, device_id=place(me ^ k, narrow), device_id_type=MESH)
        return 0

    lax.fori_loop(1, PARTS, greet, 0)
    pairs = (
        (speed_hbm, speed), (order_hbm, order), (charges_hbm, charges), (leaf_hbm, leaf_weight),
        (eval_hbm, eval_weight), (phase_hbm, phase), (mixing_hbm, mixing), (target_hbm, target),
    )
    loads = [pltpu.make_async_copy(a, b, load_sems.at[i]) for i, (a, b) in enumerate(pairs)]
    for load in loads:
        load.start()
    half = PARTS // 2
    loads[0].wait()
    speed_rows[...] = speed[...].astype(jnp.float32).reshape(half, 1, W)
    loads[1].wait()
    loads[2].wait()
    pack_rows(charges, order, packed)
    loads[3].wait()
    loads[4].wait()
    build_maps(leaf_weight, eval_weight, leaf_map, eval_map)
    pl.semaphore_wait(barrier, PARTS - 1)

    def remote(source, target, i, to):
        return pltpu.make_async_remote_copy(
            source, target.at[me], sends.at[i], recvs.at[i], device_id=place(to, narrow), device_id_type=MESH
        )

    def send_speed(k, _):
        to = me ^ k
        remote(speed_rows.at[to % half], speeds, 0, to).start()
        return 0

    def send_leaf(k, _):
        to = me ^ k
        remote(packed.at[to], leaf, 1, to).start()
        return 0

    lax.fori_loop(1, PARTS, send_speed, 0)
    lax.fori_loop(1, PARTS, send_leaf, 0)
    speeds[me] = speed_rows[me % half]
    leaf[me] = packed[me]
    others = pl.ds(0, PARTS - 1)

    def wait(ref, sem):
        pltpu.make_async_copy(ref.at[others], ref.at[others], sem).wait()

    loads[5].wait()
    wait(speeds, recvs.at[0])
    make_turns(me // half, speeds, phase, cos_p, sin_p, cos_q, sin_q)
    loads[6].wait()
    wait(leaf, recvs.at[1])
    first_levels(leaf, leaf_map, mixing, cos_p, sin_p, cos_q, sin_q, state)
    now, later = state, spare
    for level in range(3, LEVELS - 1):
        later_level(level, mixing, cos_q, sin_q, now, later)
        now, later = later, now

    def send_result(to):
        @pl.when(to != me)
        def _():
            remote(result.at[to], field, 2, to).start()

    last_level(me, send_result, mixing, eval_map, cos_p, sin_p, now, result)
    field[me] = result[me]
    loads[7].wait()
    wait(field, recvs.at[2])
    unpack_rows(field, target, out)
    store = pltpu.make_async_copy(out, out_hbm, store_sem)
    store.start()
    wait(speeds, sends.at[0])
    wait(packed, sends.at[1])
    wait(result, sends.at[2])
    store.wait()


def on_device(narrow, charges, source_order, velocity, leaf_weight, mixing, eval_weight, target_order):
    lines = charges.shape[1] // W
    half = PARTS // 2
    args = (
        charges.reshape(2, lines, W).transpose(1, 0, 2).reshape(2 * lines, W),
        source_order.reshape(lines, W),
        velocity.reshape(half, W),
        leaf_weight,
        mixing,
        eval_weight.T,
        target_order.reshape(lines, W),
        jnp.asarray(phase_map()),
    )
    chunk = pltpu.VMEM((PARTS, E, W), jnp.bfloat16)
    states = pltpu.VMEM((PAIRS, 2 * ROWS, W), jnp.bfloat16)
    rows = pltpu.VMEM((2 * lines, W), jnp.float32)
    out = pl.pallas_call(
        functools.partial(kernel, narrow),
        out_shape=jax.ShapeDtypeStruct((2 * lines, W), jnp.float32),
        in_specs=[pl.BlockSpec(memory_space=pltpu.HBM)] * len(args),
        out_specs=pl.BlockSpec(memory_space=pltpu.HBM),
        scratch_shapes=[pltpu.VMEM(a.shape, a.dtype) for a in args]
        + [
            pltpu.VMEM((half, 1, W), jnp.float32),
            pltpu.VMEM((PARTS, 1, W), jnp.float32),
            chunk,
            chunk,
            chunk,
            chunk,
            rows,
            pltpu.VMEM((W, B * W), jnp.bfloat16),
            pltpu.VMEM((B * W, W), jnp.bfloat16),
            states,
            states,
            pltpu.VMEM((len(EARLY), B, ROWS, W), jnp.bfloat16),
            pltpu.VMEM((len(EARLY), B, ROWS, W), jnp.bfloat16),
            pltpu.VMEM((LEVELS - len(EARLY), PAIRS, 2 * ROWS, W), jnp.bfloat16),
            pltpu.VMEM((LEVELS - len(EARLY), PAIRS, 2 * ROWS, W), jnp.bfloat16),
            pltpu.SemaphoreType.DMA((len(args),)),
            pltpu.SemaphoreType.DMA((3,)),
            pltpu.SemaphoreType.DMA((3,)),
            pltpu.SemaphoreType.DMA,
        ],
        compiler_params=pltpu.CompilerParams(
            has_side_effects=True, collective_id=0, vmem_limit_bytes=62 * 2**20
        ),
    )(*args)
    return out.reshape(lines, 2, W).transpose(1, 0, 2).reshape(2, lines * W)


def solution(mesh):
    both = ("wide", "narrow")
    return jax.shard_map(
        functools.partial(on_device, mesh.shape["narrow"]),
        mesh=mesh,
        in_specs=(P(None, both), P(both), P(both), P(), P(), P(), P(both)),
        out_specs=P(None, both),
        check_vma=False,
    )
```

```python
import functools
import math

import jax
import jax.numpy as jnp
import numpy as np
from jax import lax
from jax.experimental import pallas as pl
from jax.experimental.pallas import tpu as pltpu
from jax.sharding import PartitionSpec as P

MESH = pl.DeviceIdType.MESH
LEVELS = 10
PARTS = 128
E = 8
B = 8
W = 128


def half_sine_terms(count):
    w = 0.125 * (1 + np.cos(np.pi * (np.arange(64) + 0.5) / 64))
    u = np.sqrt(w)
    target = math.sqrt(2) * np.sin(np.pi * u) / u
    return np.polynomial.polynomial.polyfit(w, target, count - 1)


def phase_map():
    rank = W // 2
    nodes = np.cos(np.float32(math.pi) * (np.arange(rank, dtype=np.float32) + np.float32(0.5)) / np.float32(rank))
    rest = np.tile(nodes.astype(np.float64) * 0.5, 2)
    pieces = []
    for _ in range(3):
        pieces.append(rest.astype(jnp.bfloat16).astype(np.float64))
        rest = rest - pieces[-1]
    out = np.zeros((2, E, 2, B, B, W), np.float64)
    for b in range(B):
        out[0, :, 0, b, b, :] = pieces[0]
        out[0, :, 1, b, b, :] = pieces[1]
        out[1, :, :, b, b, :] = pieces[2]
    return out.reshape(2 * W, B * W).astype(jnp.bfloat16)


def low_half(shape):
    return lax.broadcasted_iota(jnp.int32, shape, len(shape) - 1) % W < W // 2


def half_turn(x):
    return pltpu.roll(x, W // 2, x.ndim - 1)


def slot_of(order):
    lane = lax.broadcasted_iota(jnp.int32, order.shape, 1)
    return (lane // 8) * 8 + order


def pack_rows(charges_ref, order_ref, out_ref):
    rows = 64
    half = PARTS // 2

    def body(step, _):
        at = pl.ds(pl.multiple_of(step * rows, rows), rows)
        index = slot_of(order_ref[at])
        first = charges_ref[pl.ds(pl.multiple_of(step * 2 * rows, 2 * rows), rows, stride=2)]
        second = charges_ref[pl.ds(step * 2 * rows + 1, rows, stride=2)]
        first = jnp.take_along_axis(first, index, axis=1, mode="promise_in_bounds")
        second = jnp.take_along_axis(second, index, axis=1, mode="promise_in_bounds")
        low = low_half(first.shape)
        even = jnp.where(low, first, half_turn(second)).astype(jnp.bfloat16)
        odd = jnp.where(low, half_turn(first), second).astype(jnp.bfloat16)
        out_ref[pl.ds(step * (rows // E), rows // E)] = even.reshape(rows // E, E, W)
        out_ref[pl.ds(half + step * (rows // E), rows // E)] = odd.reshape(rows // E, E, W)
        return 0

    lax.fori_loop(0, half * E // rows, body, 0)


def unpack_kernel(field_ref, order_ref, out_ref):
    rows = order_ref.shape[0]
    index = slot_of(order_ref[...])
    even = field_ref[0].astype(jnp.float32).reshape(rows, W)
    odd = field_ref[1].astype(jnp.float32).reshape(rows, W)
    low = low_half(even.shape)
    first = jnp.where(low, even, half_turn(odd))
    second = jnp.where(low, half_turn(even), odd)
    out_ref[pl.ds(0, rows, stride=2)] = jnp.take_along_axis(first, index, axis=1, mode="promise_in_bounds")
    out_ref[pl.ds(1, rows, stride=2)] = jnp.take_along_axis(second, index, axis=1, mode="promise_in_bounds")


def place(index, narrow):
    return (index // narrow, index % narrow)


def build_maps(leaf_ref, eval_ref, leaf_map_ref, eval_map_ref):
    leaf_map_ref[...] = jnp.zeros(leaf_map_ref.shape, jnp.bfloat16)
    for c in range(2):
        for b in range(B):
            rows = pl.ds(c * 64 + b * 8, 8)
            leaf_map_ref[rows, pl.ds(b * W, W)] = leaf_ref[pl.ds(c * 8, 8)]
    row = lax.broadcasted_iota(jnp.int32, (16, W), 0)
    lane = lax.broadcasted_iota(jnp.int32, (16, W), 1)
    slot = (lane // 64) * 8 + lane % 8 == row
    for b in range(B):
        pick = jnp.where(slot & (lane % 64 // 8 == b), 1.0, 0.0).astype(jnp.bfloat16)
        block = lax.dot_general(
            eval_ref[...], pick, (((0,), (0,)), ((), ())), preferred_element_type=jnp.float32
        )
        eval_map_ref[pl.ds(b * W, W)] = block.astype(jnp.bfloat16)


def rotate(pre, cosine, sine):
    return pre * cosine + half_turn(pre) * sine


def level_map(mixing_ref, level):
    return jnp.concatenate(
        [jnp.concatenate([mixing_ref[level, j, i] for i in range(2)], axis=0) for j in range(2)], axis=1
    )


def mix(near, far, maps):
    pre = jnp.dot(jnp.concatenate([near, far], axis=1), maps, preferred_element_type=jnp.float32)
    return [pre[:, :W], pre[:, W:]]


def pair_up(even, odd):
    rows = even.shape[0]
    both = jnp.concatenate([even.reshape(rows // E, E, W), odd.reshape(rows // E, E, W)], axis=1)
    return both.reshape(2 * rows, W)


TURN_ND, FIRST_ND, LATER_PAIRS, LAST_ND = 8, 64, 2, 16
PAIRS = B // 2
ROWS = PARTS * E
EARLY = {0: 0, 1: 1, LEVELS - 1: 2}


def make_turns(me, arrived, speed_ref, phase_ref, cos_p, sin_p, cos_q, sin_q):
    terms = half_sine_terms(5)
    nd = TURN_ND
    rows = nd * E

    def body(count, _):
        arrived(count)
        step = count ^ me // nd
        at = pl.ds(pl.multiple_of(step * nd, nd), nd)
        speeds = jnp.broadcast_to(speed_ref[at], (nd, E, W)).reshape(rows, W)
        lane = lax.broadcasted_iota(jnp.int32, (rows, W), 1)
        row = lax.broadcasted_iota(jnp.int32, (rows, W), 0)
        mine = (lane // 16 == row % E) & (lane // B % 2 == me // (PARTS // 2))
        own = jnp.where(mine, speeds, 0.0)
        operand = jnp.concatenate([own + pltpu.roll(own, B, 1), own], axis=1).astype(jnp.bfloat16)
        counts = jnp.dot(operand, phase_ref[...], preferred_element_type=jnp.float32)
        low = low_half((rows, W))
        quarter = jnp.where(low, 0.0, 0.25)
        rows_at = pl.ds(pl.multiple_of(step * rows, rows), rows)
        wide_at = pl.ds(pl.multiple_of(step * rows * 2, rows * 2), rows * 2)
        for pair in range(PAIRS):
            cosine, sine, twice = [], [], []
            for b in (2 * pair, 2 * pair + 1):
                u = counts[:, b * W : (b + 1) * W] - quarter
                u = u - jnp.round(u)
                w = u * u
                p = w * jnp.float32(terms[4]) + jnp.float32(terms[3])
                for k in (2, 1, 0):
                    p = p * w + jnp.float32(terms[k])
                s = u * p
                t = 1.0 - s * s
                other = half_turn(t)
                cosine.append(jnp.where(low, t, other))
                sine.append(jnp.where(low, -other, t))
                twice.append(cosine[-1] + cosine[-1])
            last = None
            for level in range(LEVELS):
                for now, early, late in ((cosine, cos_p, cos_q), (sine, sin_p, sin_q)):
                    if level in EARLY:
                        for i in range(2):
                            early[EARLY[level], 2 * pair + i, rows_at] = now[i].astype(jnp.bfloat16)
                    else:
                        late[level - 2, pair, wide_at] = pair_up(now[0], now[1]).astype(jnp.bfloat16)
                if level == LEVELS - 1:
                    break
                if last is None:
                    after = [twice[i] * cosine[i] - 1.0 for i in range(2)], [twice[i] * sine[i] for i in range(2)]
                else:
                    after = [
                        [twice[i] * now[i] - before[i] for i in range(2)]
                        for now, before in ((cosine, last[0]), (sine, last[1]))
                    ]
                last = cosine, sine
                cosine, sine = after
        return 0

    lax.fori_loop(0, PARTS // nd, body, 0)


def first_levels(leaf_ref, leaf_map_ref, mixing_ref, cos_p, sin_p, cos_q, sin_q, state):
    nd = FIRST_ND
    rows = nd * E

    def body(step, _):
        at = pl.ds(pl.multiple_of(step * nd, nd), nd)
        rows_at = pl.ds(pl.multiple_of(step * rows, rows), rows)
        wide_at = pl.ds(pl.multiple_of(step * rows * 2, rows * 2), rows * 2)
        leaf = leaf_ref[at].reshape(rows, W)
        boxes = [None] * B
        maps = level_map(mixing_ref, 0)
        for pair in range(PAIRS):
            lanes = pl.ds(pair * 2 * W, 2 * W)
            spread = jnp.dot(leaf, leaf_map_ref[:, lanes], preferred_element_type=jnp.float32)
            pre = jnp.dot(spread.astype(jnp.bfloat16), maps, preferred_element_type=jnp.float32)
            for i in range(2):
                b = 2 * pair + i
                boxes[b] = rotate(pre[:, i * W : (i + 1) * W].astype(jnp.bfloat16), cos_p[0, b, rows_at], sin_p[0, b, rows_at])
        maps = level_map(mixing_ref, 1)
        for b in (0, 1, 4, 5):
            for i, pre in enumerate(mix(boxes[b], boxes[b + 2], maps)):
                box = b + 2 * i
                boxes[box] = rotate(pre.astype(jnp.bfloat16), cos_p[1, box, rows_at], sin_p[1, box, rows_at])
        maps = level_map(mixing_ref, 2)
        for pair in range(2):
            pres = [mix(boxes[2 * pair + i], boxes[2 * pair + i + 4], maps) for i in range(2)]
            for i in range(2):
                pre = pair_up(pres[0][i], pres[1][i]).astype(jnp.bfloat16)
                unit = pair + 2 * i
                state[unit, wide_at] = rotate(pre, cos_q[0, unit, wide_at], sin_q[0, unit, wide_at])
        return 0

    lax.fori_loop(0, PARTS // nd, body, 0)


def later_level(level, mixing_ref, cos_q, sin_q, source, target):
    stride = 2 * E << (level - 3)
    starts = range(0, 2 * ROWS, 2 * stride)

    def body(step, _):
        maps = level_map(mixing_ref, level)
        for i in range(LATER_PAIRS):
            pair = step * LATER_PAIRS + i
            near = jnp.concatenate([source[pair, pl.ds(at, stride)] for at in starts], axis=0)
            far = jnp.concatenate([source[pair, pl.ds(at + stride, stride)] for at in starts], axis=0)
            for side, pre in enumerate(mix(near, far, maps)):
                for n, at in enumerate(starts):
                    rows_at = pl.ds(at + side * stride, stride)
                    part = pre[n * stride : (n + 1) * stride].astype(jnp.bfloat16)
                    target[pair, rows_at] = rotate(
                        part, cos_q[level - 2, pair, rows_at], sin_q[level - 2, pair, rows_at]
                    )
        return 0

    lax.fori_loop(0, PAIRS // LATER_PAIRS, body, 0)


def last_level(me, send, mixing_ref, eval_map_ref, cos_p, sin_p, state, out_ref):
    level = LEVELS - 1
    nd = LAST_ND
    rows = nd * E
    steps = PARTS // 2 // nd

    def body(count, _):
        step = (count + me // nd) % steps
        maps = level_map(mixing_ref, level)
        boxes = [[], []]
        wide = [pl.ds(pl.multiple_of(step * 2 * rows + side * ROWS, 2 * rows), 2 * rows) for side in range(2)]
        for pair in range(PAIRS):
            for side, pre in enumerate(mix(state[pair, wide[0]], state[pair, wide[1]], maps)):
                own = pre.reshape(nd, 2, E, W)
                rows_at = pl.ds(pl.multiple_of(step * rows + side * (ROWS // 2), rows), rows)
                for i in range(2):
                    box = own[:, i].reshape(rows, W).astype(jnp.bfloat16)
                    at = EARLY[level], 2 * pair + i, rows_at
                    boxes[side].append(rotate(box, cos_p[at], sin_p[at]))
        for side in range(2):
            values = jnp.dot(
                jnp.concatenate(boxes[side], axis=1), eval_map_ref[...], preferred_element_type=jnp.float32
            )
            at = pl.ds(step * nd + side * (PARTS // 2), nd)
            out_ref[at] = values.astype(jnp.bfloat16).reshape(nd, E, W)

        def one(i, _):
            for side in range(2):
                send(step * nd + side * (PARTS // 2) + ((i + me) % nd))
            return 0

        lax.fori_loop(0, nd, one, 0)
        return 0

    lax.fori_loop(0, steps, body, 0)


def kernel(
    narrow, charges_hbm, order_hbm, speed_hbm, leaf_hbm, mixing_hbm, eval_hbm, phase_hbm, field,
    charges, order, speed, leaf_weight, mixing, eval_weight, phase,
    speed_rows, speeds, packed, leaf, result, leaf_map, eval_map, state, spare, cos_p, sin_p, cos_q, sin_q,
    load_sems, sends, recvs, speed_recvs, own_sem,
):
    me = lax.axis_index("wide") * narrow + lax.axis_index("narrow")
    barrier = pltpu.get_barrier_semaphore()

    def greet(k, _):
        pl.semaphore_signal(barrier, inc=1, device_id=place(me ^ k, narrow), device_id_type=MESH)
        return 0

    lax.fori_loop(1, PARTS, greet, 0)
    pairs = (
        (speed_hbm, speed), (order_hbm, order), (charges_hbm, charges), (leaf_hbm, leaf_weight),
        (eval_hbm, eval_weight), (phase_hbm, phase), (mixing_hbm, mixing),
    )
    loads = [pltpu.make_async_copy(a, b, load_sems.at[i]) for i, (a, b) in enumerate(pairs)]
    for load in loads:
        load.start()
    half = PARTS // 2
    loads[0].wait()
    speed_rows[...] = speed[...].astype(jnp.float32).reshape(half, 1, W)
    loads[1].wait()
    loads[2].wait()
    pack_rows(charges, order, packed)
    loads[3].wait()
    loads[4].wait()
    build_maps(leaf_weight, eval_weight, leaf_map, eval_map)
    pl.semaphore_wait(barrier, PARTS - 1)

    def remote(source, target, i, to, recv):
        return pltpu.make_async_remote_copy(
            source, target.at[me], sends.at[i], recv, device_id=place(to, narrow), device_id_type=MESH
        )

    def send_speed(k, _):
        to = me ^ k
        remote(speed_rows.at[to % half], speeds, 0, to, speed_recvs.at[k // TURN_ND]).start()
        return 0

    def send_leaf(k, _):
        to = me ^ k
        remote(packed.at[to], leaf, 1, to, recvs.at[0]).start()
        return 0

    lax.fori_loop(1, PARTS, send_speed, 0)
    lax.fori_loop(1, PARTS, send_leaf, 0)
    speeds[me] = speed_rows[me % half]
    leaf[me] = packed[me]

    def wait(ref, sem, count=PARTS - 1):
        some = pl.ds(0, count)
        pltpu.make_async_copy(ref.at[some], ref.at[some], sem).wait()

    def arrived(count):
        @pl.when(count == 0)
        def _():
            wait(speeds, speed_recvs.at[count], TURN_ND - 1)

        @pl.when(count > 0)
        def _():
            wait(speeds, speed_recvs.at[count], TURN_ND)

    loads[5].wait()
    make_turns(me, arrived, speeds, phase, cos_p, sin_p, cos_q, sin_q)
    loads[6].wait()
    wait(leaf, recvs.at[0])
    first_levels(leaf, leaf_map, mixing, cos_p, sin_p, cos_q, sin_q, state)
    now, later = state, spare
    for level in range(3, LEVELS - 1):
        later_level(level, mixing, cos_q, sin_q, now, later)
        now, later = later, now

    def send_result(to):
        @pl.when(to != me)
        def _():
            remote(result.at[to], field, 2, to, recvs.at[1]).start()

    last_level(me, send_result, mixing, eval_map, cos_p, sin_p, now, result)
    own = pltpu.make_async_copy(result.at[me], field.at[me], own_sem)
    own.start()
    wait(speeds, sends.at[0])
    wait(packed, sends.at[1])
    wait(result, recvs.at[1])
    wait(result, sends.at[2])
    own.wait()


def on_device(narrow, charges, source_order, velocity, leaf_weight, mixing, eval_weight, target_order):
    lines = charges.shape[1] // W
    half = PARTS // 2
    args = (
        charges.reshape(2, lines, W).transpose(1, 0, 2).reshape(2 * lines, W),
        source_order.reshape(lines, W),
        velocity.reshape(half, W),
        leaf_weight,
        mixing,
        eval_weight.T,
        jnp.asarray(phase_map()),
    )
    chunk = pltpu.VMEM((PARTS, E, W), jnp.bfloat16)
    states = pltpu.VMEM((PAIRS, 2 * ROWS, W), jnp.bfloat16)
    field = pl.pallas_call(
        functools.partial(kernel, narrow),
        out_shape=jax.ShapeDtypeStruct((PARTS, E, W), jnp.bfloat16),
        in_specs=[pl.BlockSpec(memory_space=pltpu.HBM)] * len(args),
        out_specs=pl.BlockSpec(memory_space=pltpu.HBM),
        scratch_shapes=[pltpu.VMEM(a.shape, a.dtype) for a in args]
        + [
            pltpu.VMEM((half, 1, W), jnp.float32),
            pltpu.VMEM((PARTS, 1, W), jnp.float32),
            chunk,
            chunk,
            chunk,
            pltpu.VMEM((W, B * W), jnp.bfloat16),
            pltpu.VMEM((B * W, W), jnp.bfloat16),
            states,
            states,
            pltpu.VMEM((len(EARLY), B, ROWS, W), jnp.bfloat16),
            pltpu.VMEM((len(EARLY), B, ROWS, W), jnp.bfloat16),
            pltpu.VMEM((LEVELS - len(EARLY), PAIRS, 2 * ROWS, W), jnp.bfloat16),
            pltpu.VMEM((LEVELS - len(EARLY), PAIRS, 2 * ROWS, W), jnp.bfloat16),
            pltpu.SemaphoreType.DMA((len(args),)),
            pltpu.SemaphoreType.DMA((3,)),
            pltpu.SemaphoreType.DMA((2,)),
            pltpu.SemaphoreType.DMA((PARTS // TURN_ND,)),
            pltpu.SemaphoreType.DMA,
        ],
        compiler_params=pltpu.CompilerParams(
            has_side_effects=True, collective_id=0, vmem_limit_bytes=62 * 2**20
        ),
    )(*args)
    blocks = 4
    out = pl.pallas_call(
        unpack_kernel,
        grid=(blocks,),
        out_shape=jax.ShapeDtypeStruct((2 * lines, W), jnp.float32),
        in_specs=[
            pl.BlockSpec((2, half // blocks, E, W), lambda i: (0, i, 0, 0)),
            pl.BlockSpec((lines // blocks, W), lambda i: (i, 0)),
        ],
        out_specs=pl.BlockSpec((2 * lines // blocks, W), lambda i: (i, 0)),
    )(field.reshape(2, half, E, W), target_order.reshape(lines, W))
    return out.reshape(lines, 2, W).transpose(1, 0, 2).reshape(2, lines * W)


def solution(mesh):
    both = ("wide", "narrow")
    return jax.shard_map(
        functools.partial(on_device, mesh.shape["narrow"]),
        mesh=mesh,
        in_specs=(P(None, both), P(both), P(both), P(), P(), P(), P(both)),
        out_specs=P(None, both),
        check_vma=False,
    )
```

```python
import functools
import math

import jax
import jax.numpy as jnp
import numpy as np
from jax import lax
from jax.experimental import pallas as pl
from jax.experimental.pallas import tpu as pltpu
from jax.sharding import PartitionSpec as P

MESH = pl.DeviceIdType.MESH
LEVELS = 10
PARTS = 128
E = 8
B = 8
W = 128


def half_sine_terms(count):
    w = 0.125 * (1 + np.cos(np.pi * (np.arange(64) + 0.5) / 64))
    u = np.sqrt(w)
    target = math.sqrt(2) * np.sin(np.pi * u) / u
    return np.polynomial.polynomial.polyfit(w, target, count - 1)


def phase_map():
    rank = W // 2
    nodes = np.cos(np.float32(math.pi) * (np.arange(rank, dtype=np.float32) + np.float32(0.5)) / np.float32(rank))
    rest = np.tile(nodes.astype(np.float64) * 0.5, 2)
    pieces = []
    for _ in range(3):
        pieces.append(rest.astype(jnp.bfloat16).astype(np.float64))
        rest = rest - pieces[-1]
    out = np.zeros((2, E, 2, B, B, W), np.float64)
    for b in range(B):
        out[0, :, 0, b, b, :] = pieces[0]
        out[0, :, 1, b, b, :] = pieces[1]
        out[1, :, :, b, b, :] = pieces[2]
    return out.reshape(2 * W, B * W).astype(jnp.bfloat16)


def low_half(shape):
    return lax.broadcasted_iota(jnp.int32, shape, len(shape) - 1) % W < W // 2


def half_turn(x):
    return pltpu.roll(x, W // 2, x.ndim - 1)


def slot_of(order):
    lane = lax.broadcasted_iota(jnp.int32, order.shape, 1)
    return (lane // 8) * 8 + order


def pack_rows(charges_ref, order_ref, out_ref):
    rows = 64
    half = PARTS // 2

    def body(step, _):
        at = pl.ds(pl.multiple_of(step * rows, rows), rows)
        index = slot_of(order_ref[at])
        first = charges_ref[pl.ds(pl.multiple_of(step * 2 * rows, 2 * rows), rows, stride=2)]
        second = charges_ref[pl.ds(step * 2 * rows + 1, rows, stride=2)]
        first = jnp.take_along_axis(first, index, axis=1, mode="promise_in_bounds")
        second = jnp.take_along_axis(second, index, axis=1, mode="promise_in_bounds")
        low = low_half(first.shape)
        even = jnp.where(low, first, half_turn(second)).astype(jnp.bfloat16)
        odd = jnp.where(low, half_turn(first), second).astype(jnp.bfloat16)
        out_ref[pl.ds(step * (rows // E), rows // E)] = even.reshape(rows // E, E, W)
        out_ref[pl.ds(half + step * (rows // E), rows // E)] = odd.reshape(rows // E, E, W)
        return 0

    lax.fori_loop(0, half * E // rows, body, 0)


def unpack_kernel(field_ref, order_ref, out_ref):
    rows = order_ref.shape[0]
    index = slot_of(order_ref[...])
    even = field_ref[0].astype(jnp.float32).reshape(rows, W)
    odd = field_ref[1].astype(jnp.float32).reshape(rows, W)
    low = low_half(even.shape)
    first = jnp.where(low, even, half_turn(odd))
    second = jnp.where(low, half_turn(even), odd)
    out_ref[pl.ds(0, rows, stride=2)] = jnp.take_along_axis(first, index, axis=1, mode="promise_in_bounds")
    out_ref[pl.ds(1, rows, stride=2)] = jnp.take_along_axis(second, index, axis=1, mode="promise_in_bounds")


def place(index, narrow):
    return (index // narrow, index % narrow)


def build_maps(leaf_ref, eval_ref, leaf_map_ref, eval_map_ref):
    leaf_map_ref[...] = jnp.zeros(leaf_map_ref.shape, jnp.bfloat16)
    for c in range(2):
        for b in range(B):
            rows = pl.ds(c * 64 + b * 8, 8)
            leaf_map_ref[rows, pl.ds(b * W, W)] = leaf_ref[pl.ds(c * 8, 8)]
    row = lax.broadcasted_iota(jnp.int32, (16, W), 0)
    lane = lax.broadcasted_iota(jnp.int32, (16, W), 1)
    slot = (lane // 64) * 8 + lane % 8 == row
    for b in range(B):
        pick = jnp.where(slot & (lane % 64 // 8 == b), 1.0, 0.0).astype(jnp.bfloat16)
        block = lax.dot_general(
            eval_ref[...], pick, (((0,), (0,)), ((), ())), preferred_element_type=jnp.float32
        )
        eval_map_ref[pl.ds(b * W, W)] = block.astype(jnp.bfloat16)


def rotate(pre, cosine, sine):
    return pre * cosine + half_turn(pre) * sine


def level_map(mixing_ref, level):
    return jnp.concatenate(
        [jnp.concatenate([mixing_ref[level, j, i] for i in range(2)], axis=0) for j in range(2)], axis=1
    )


def mix(near, far, maps):
    pre = jnp.dot(jnp.concatenate([near, far], axis=1), maps, preferred_element_type=jnp.float32)
    return [pre[:, :W], pre[:, W:]]


def pair_up(even, odd):
    rows = even.shape[0]
    both = jnp.concatenate([even.reshape(rows // E, E, W), odd.reshape(rows // E, E, W)], axis=1)
    return both.reshape(2 * rows, W)


TURN_ND, FIRST_ND, LATER_PAIRS, LAST_ND = 16, 128, 2, 32
PAIRS = B // 2
ROWS = PARTS * E
EARLY = {0: 0, 1: 1, LEVELS - 1: 2}


def make_turns(me, arrived, speed_ref, phase_ref, cos_p, sin_p, cos_q, sin_q):
    terms = half_sine_terms(5)
    nd = TURN_ND
    rows = nd * E

    def body(count, _):
        arrived(count)
        step = count ^ me // nd
        at = pl.ds(pl.multiple_of(step * nd, nd), nd)
        speeds = jnp.broadcast_to(speed_ref[at], (nd, E, W)).reshape(rows, W)
        lane = lax.broadcasted_iota(jnp.int32, (rows, W), 1)
        row = lax.broadcasted_iota(jnp.int32, (rows, W), 0)
        mine = (lane // 16 == row % E) & (lane // B % 2 == me // (PARTS // 2))
        own = jnp.where(mine, speeds, 0.0)
        operand = jnp.concatenate([own + pltpu.roll(own, B, 1), own], axis=1).astype(jnp.bfloat16)
        counts = jnp.dot(operand, phase_ref[...], preferred_element_type=jnp.float32)
        low = low_half((rows, W))
        quarter = jnp.where(low, 0.0, 0.25)
        rows_at = pl.ds(pl.multiple_of(step * rows, rows), rows)
        wide_at = pl.ds(pl.multiple_of(step * rows * 2, rows * 2), rows * 2)
        for pair in range(PAIRS):
            cosine, sine, twice = [], [], []
            for b in (2 * pair, 2 * pair + 1):
                u = counts[:, b * W : (b + 1) * W] - quarter
                u = u - jnp.round(u)
                w = u * u
                p = w * jnp.float32(terms[4]) + jnp.float32(terms[3])
                for k in (2, 1, 0):
                    p = p * w + jnp.float32(terms[k])
                s = u * p
                t = 1.0 - s * s
                other = half_turn(t)
                cosine.append(jnp.where(low, t, other))
                sine.append(jnp.where(low, -other, t))
                twice.append(cosine[-1] + cosine[-1])
            last = None
            for level in range(LEVELS):
                for now, early, late in ((cosine, cos_p, cos_q), (sine, sin_p, sin_q)):
                    if level in EARLY:
                        for i in range(2):
                            early[EARLY[level], 2 * pair + i, rows_at] = now[i].astype(jnp.bfloat16)
                    else:
                        late[level - 2, pair, wide_at] = pair_up(now[0], now[1]).astype(jnp.bfloat16)
                if level == LEVELS - 1:
                    break
                if last is None:
                    after = [twice[i] * cosine[i] - 1.0 for i in range(2)], [twice[i] * sine[i] for i in range(2)]
                else:
                    after = [
                        [twice[i] * now[i] - before[i] for i in range(2)]
                        for now, before in ((cosine, last[0]), (sine, last[1]))
                    ]
                last = cosine, sine
                cosine, sine = after
        return 0

    lax.fori_loop(0, PARTS // nd, body, 0)


def first_levels(leaf_ref, leaf_map_ref, mixing_ref, cos_p, sin_p, cos_q, sin_q, state):
    nd = FIRST_ND
    rows = nd * E

    def body(step, _):
        at = pl.ds(pl.multiple_of(step * nd, nd), nd)
        rows_at = pl.ds(pl.multiple_of(step * rows, rows), rows)
        wide_at = pl.ds(pl.multiple_of(step * rows * 2, rows * 2), rows * 2)
        leaf = leaf_ref[at].reshape(rows, W)
        boxes = [None] * B
        maps = level_map(mixing_ref, 0)
        for pair in range(PAIRS):
            lanes = pl.ds(pair * 2 * W, 2 * W)
            spread = jnp.dot(leaf, leaf_map_ref[:, lanes], preferred_element_type=jnp.float32)
            pre = jnp.dot(spread.astype(jnp.bfloat16), maps, preferred_element_type=jnp.float32)
            for i in range(2):
                b = 2 * pair + i
                boxes[b] = rotate(pre[:, i * W : (i + 1) * W].astype(jnp.bfloat16), cos_p[0, b, rows_at], sin_p[0, b, rows_at])
        maps = level_map(mixing_ref, 1)
        for b in (0, 1, 4, 5):
            for i, pre in enumerate(mix(boxes[b], boxes[b + 2], maps)):
                box = b + 2 * i
                boxes[box] = rotate(pre.astype(jnp.bfloat16), cos_p[1, box, rows_at], sin_p[1, box, rows_at])
        maps = level_map(mixing_ref, 2)
        for pair in range(2):
            pres = [mix(boxes[2 * pair + i], boxes[2 * pair + i + 4], maps) for i in range(2)]
            for i in range(2):
                pre = pair_up(pres[0][i], pres[1][i]).astype(jnp.bfloat16)
                unit = pair + 2 * i
                state[unit, wide_at] = rotate(pre, cos_q[0, unit, wide_at], sin_q[0, unit, wide_at])
        return 0

    lax.fori_loop(0, PARTS // nd, body, 0)


def later_level(level, mixing_ref, cos_q, sin_q, source, target):
    stride = 2 * E << (level - 3)
    starts = range(0, 2 * ROWS, 2 * stride)

    def body(step, _):
        maps = level_map(mixing_ref, level)
        for i in range(LATER_PAIRS):
            pair = step * LATER_PAIRS + i
            near = jnp.concatenate([source[pair, pl.ds(at, stride)] for at in starts], axis=0)
            far = jnp.concatenate([source[pair, pl.ds(at + stride, stride)] for at in starts], axis=0)
            for side, pre in enumerate(mix(near, far, maps)):
                for n, at in enumerate(starts):
                    rows_at = pl.ds(at + side * stride, stride)
                    part = pre[n * stride : (n + 1) * stride].astype(jnp.bfloat16)
                    target[pair, rows_at] = rotate(
                        part, cos_q[level - 2, pair, rows_at], sin_q[level - 2, pair, rows_at]
                    )
        return 0

    lax.fori_loop(0, PAIRS // LATER_PAIRS, body, 0)


def last_level(me, send, mixing_ref, eval_map_ref, cos_p, sin_p, state, out_ref):
    level = LEVELS - 1
    nd = LAST_ND
    rows = nd * E
    steps = PARTS // 2 // nd

    def body(count, _):
        step = (count + me // nd) % steps
        maps = level_map(mixing_ref, level)
        boxes = [[], []]
        wide = [pl.ds(pl.multiple_of(step * 2 * rows + side * ROWS, 2 * rows), 2 * rows) for side in range(2)]
        for pair in range(PAIRS):
            for side, pre in enumerate(mix(state[pair, wide[0]], state[pair, wide[1]], maps)):
                own = pre.reshape(nd, 2, E, W)
                rows_at = pl.ds(pl.multiple_of(step * rows + side * (ROWS // 2), rows), rows)
                for i in range(2):
                    box = own[:, i].reshape(rows, W).astype(jnp.bfloat16)
                    at = EARLY[level], 2 * pair + i, rows_at
                    boxes[side].append(rotate(box, cos_p[at], sin_p[at]))
        for side in range(2):
            values = jnp.dot(
                jnp.concatenate(boxes[side], axis=1), eval_map_ref[...], preferred_element_type=jnp.float32
            )
            at = pl.ds(step * nd + side * (PARTS // 2), nd)
            out_ref[at] = values.astype(jnp.bfloat16).reshape(nd, E, W)

        def one(i, _):
            for side in range(2):
                send(step * nd + side * (PARTS // 2) + ((i + me) % nd))
            return 0

        lax.fori_loop(0, nd, one, 0)
        return 0

    lax.fori_loop(0, steps, body, 0)


def kernel(
    narrow, charges_hbm, order_hbm, speed_hbm, leaf_hbm, mixing_hbm, eval_hbm, phase_hbm, field,
    charges, order, speed, leaf_weight, mixing, eval_weight, phase,
    speed_rows, speeds, packed, leaf, result, leaf_map, eval_map, state, spare, cos_p, sin_p, cos_q, sin_q,
    load_sems, sends, recvs, speed_recvs, own_sem,
):
    me = lax.axis_index("wide") * narrow + lax.axis_index("narrow")
    barrier = pltpu.get_barrier_semaphore()

    def greet(k, _):
        pl.semaphore_signal(barrier, inc=1, device_id=place(me ^ k, narrow), device_id_type=MESH)
        return 0

    lax.fori_loop(1, PARTS, greet, 0)
    pairs = (
        (speed_hbm, speed), (order_hbm, order), (charges_hbm, charges), (leaf_hbm, leaf_weight),
        (eval_hbm, eval_weight), (phase_hbm, phase), (mixing_hbm, mixing),
    )
    loads = [pltpu.make_async_copy(a, b, load_sems.at[i]) for i, (a, b) in enumerate(pairs)]
    for load in loads:
        load.start()
    half = PARTS // 2
    loads[0].wait()
    speed_rows[...] = speed[...].astype(jnp.float32).reshape(half, 1, W)
    loads[1].wait()
    loads[2].wait()
    pack_rows(charges, order, packed)
    loads[3].wait()
    loads[4].wait()
    build_maps(leaf_weight, eval_weight, leaf_map, eval_map)
    pl.semaphore_wait(barrier, PARTS - 1)

    def remote(source, target, i, to, recv):
        return pltpu.make_async_remote_copy(
            source, target.at[me], sends.at[i], recv, device_id=place(to, narrow), device_id_type=MESH
        )

    def send_speed(k, _):
        to = me ^ k
        remote(speed_rows.at[to % half], speeds, 0, to, speed_recvs.at[k // TURN_ND]).start()
        return 0

    def send_leaf(k, _):
        to = me ^ k
        remote(packed.at[to], leaf, 1, to, recvs.at[0]).start()
        return 0

    lax.fori_loop(1, PARTS, send_speed, 0)
    lax.fori_loop(1, PARTS, send_leaf, 0)
    speeds[me] = speed_rows[me % half]
    leaf[me] = packed[me]

    def wait(ref, sem, count=PARTS - 1):
        some = pl.ds(0, count)
        pltpu.make_async_copy(ref.at[some], ref.at[some], sem).wait()

    def arrived(count):
        @pl.when(count == 0)
        def _():
            wait(speeds, speed_recvs.at[count], TURN_ND - 1)

        @pl.when(count > 0)
        def _():
            wait(speeds, speed_recvs.at[count], TURN_ND)

    loads[5].wait()
    make_turns(me, arrived, speeds, phase, cos_p, sin_p, cos_q, sin_q)
    loads[6].wait()
    wait(leaf, recvs.at[0])
    first_levels(leaf, leaf_map, mixing, cos_p, sin_p, cos_q, sin_q, state)
    now, later = state, spare
    for level in range(3, LEVELS - 1):
        later_level(level, mixing, cos_q, sin_q, now, later)
        now, later = later, now

    def send_result(to):
        @pl.when(to != me)
        def _():
            remote(result.at[to], field, 2, to, recvs.at[1]).start()

    last_level(me, send_result, mixing, eval_map, cos_p, sin_p, now, result)
    own = pltpu.make_async_copy(result.at[me], field.at[me], own_sem)
    own.start()
    wait(speeds, sends.at[0])
    wait(packed, sends.at[1])
    wait(result, recvs.at[1])
    wait(result, sends.at[2])
    own.wait()


def on_device(narrow, charges, source_order, velocity, leaf_weight, mixing, eval_weight, target_order):
    lines = charges.shape[1] // W
    half = PARTS // 2
    args = (
        charges.reshape(2, lines, W).transpose(1, 0, 2).reshape(2 * lines, W),
        source_order.reshape(lines, W),
        velocity.reshape(half, W),
        leaf_weight,
        mixing,
        eval_weight.T,
        jnp.asarray(phase_map()),
    )
    chunk = pltpu.VMEM((PARTS, E, W), jnp.bfloat16)
    states = pltpu.VMEM((PAIRS, 2 * ROWS, W), jnp.bfloat16)
    field = pl.pallas_call(
        functools.partial(kernel, narrow),
        out_shape=jax.ShapeDtypeStruct((PARTS, E, W), jnp.bfloat16),
        in_specs=[pl.BlockSpec(memory_space=pltpu.HBM)] * len(args),
        out_specs=pl.BlockSpec(memory_space=pltpu.HBM),
        scratch_shapes=[pltpu.VMEM(a.shape, a.dtype) for a in args]
        + [
            pltpu.VMEM((half, 1, W), jnp.float32),
            pltpu.VMEM((PARTS, 1, W), jnp.float32),
            chunk,
            chunk,
            chunk,
            pltpu.VMEM((W, B * W), jnp.bfloat16),
            pltpu.VMEM((B * W, W), jnp.bfloat16),
            states,
            states,
            pltpu.VMEM((len(EARLY), B, ROWS, W), jnp.bfloat16),
            pltpu.VMEM((len(EARLY), B, ROWS, W), jnp.bfloat16),
            pltpu.VMEM((LEVELS - len(EARLY), PAIRS, 2 * ROWS, W), jnp.bfloat16),
            pltpu.VMEM((LEVELS - len(EARLY), PAIRS, 2 * ROWS, W), jnp.bfloat16),
            pltpu.SemaphoreType.DMA((len(args),)),
            pltpu.SemaphoreType.DMA((3,)),
            pltpu.SemaphoreType.DMA((2,)),
            pltpu.SemaphoreType.DMA((PARTS // TURN_ND,)),
            pltpu.SemaphoreType.DMA,
        ],
        compiler_params=pltpu.CompilerParams(
            has_side_effects=True, collective_id=0, vmem_limit_bytes=62 * 2**20
        ),
    )(*args)
    blocks = 2
    out = pl.pallas_call(
        unpack_kernel,
        grid=(blocks,),
        out_shape=jax.ShapeDtypeStruct((2 * lines, W), jnp.float32),
        in_specs=[
            pl.BlockSpec((2, half // blocks, E, W), lambda i: (0, i, 0, 0)),
            pl.BlockSpec((lines // blocks, W), lambda i: (i, 0)),
        ],
        out_specs=pl.BlockSpec((2 * lines // blocks, W), lambda i: (i, 0)),
    )(field.reshape(2, half, E, W), target_order.reshape(lines, W))
    return out.reshape(lines, 2, W).transpose(1, 0, 2).reshape(2, lines * W)


def solution(mesh):
    both = ("wide", "narrow")
    return jax.shard_map(
        functools.partial(on_device, mesh.shape["narrow"]),
        mesh=mesh,
        in_specs=(P(None, both), P(both), P(both), P(), P(), P(), P(both)),
        out_specs=P(None, both),
        check_vma=False,
    )
```

```python
import functools
import math

import jax
import jax.numpy as jnp
import numpy as np
from jax import lax
from jax.experimental import pallas as pl
from jax.experimental.pallas import tpu as pltpu
from jax.sharding import PartitionSpec as P

MESH = pl.DeviceIdType.MESH
LEVELS = 10
PARTS = 128
E = 8
B = 8
W = 128


def half_sine_terms(count):
    w = 0.125 * (1 + np.cos(np.pi * (np.arange(64) + 0.5) / 64))
    u = np.sqrt(w)
    target = math.sqrt(2) * np.sin(np.pi * u) / u
    return np.polynomial.polynomial.polyfit(w, target, count - 1)


def phase_map():
    rank = W // 2
    nodes = np.cos(np.float32(math.pi) * (np.arange(rank, dtype=np.float32) + np.float32(0.5)) / np.float32(rank))
    rest = np.tile(nodes.astype(np.float64) * 0.5, 2)
    pieces = []
    for _ in range(3):
        pieces.append(rest.astype(jnp.bfloat16).astype(np.float64))
        rest = rest - pieces[-1]
    out = np.zeros((2, E, 2, B, B, W), np.float64)
    for b in range(B):
        out[0, :, 0, b, b, :] = pieces[0]
        out[0, :, 1, b, b, :] = pieces[1]
        out[1, :, :, b, b, :] = pieces[2]
    return out.reshape(2 * W, B * W).astype(jnp.bfloat16)


def low_half(shape):
    return lax.broadcasted_iota(jnp.int32, shape, len(shape) - 1) % W < W // 2


def half_turn(x):
    return pltpu.roll(x, W // 2, x.ndim - 1)


def slot_of(order):
    lane = lax.broadcasted_iota(jnp.int32, order.shape, 1)
    return (lane // 8) * 8 + order


def pack_rows(charges_ref, order_ref, out_ref):
    rows = 64
    half = PARTS // 2

    def body(step, _):
        at = pl.ds(pl.multiple_of(step * rows, rows), rows)
        index = slot_of(order_ref[at])
        first = charges_ref[pl.ds(pl.multiple_of(step * 2 * rows, 2 * rows), rows, stride=2)]
        second = charges_ref[pl.ds(step * 2 * rows + 1, rows, stride=2)]
        first = jnp.take_along_axis(first, index, axis=1, mode="promise_in_bounds")
        second = jnp.take_along_axis(second, index, axis=1, mode="promise_in_bounds")
        low = low_half(first.shape)
        even = jnp.where(low, first, half_turn(second)).astype(jnp.bfloat16)
        odd = jnp.where(low, half_turn(first), second).astype(jnp.bfloat16)
        out_ref[pl.ds(step * (rows // E), rows // E)] = even.reshape(rows // E, E, W)
        out_ref[pl.ds(half + step * (rows // E), rows // E)] = odd.reshape(rows // E, E, W)
        return 0

    lax.fori_loop(0, half * E // rows, body, 0)


def unpack_kernel(field_ref, order_ref, out_ref):
    rows = order_ref.shape[0]
    index = slot_of(order_ref[...])
    even = field_ref[0].astype(jnp.float32).reshape(rows, W)
    odd = field_ref[1].astype(jnp.float32).reshape(rows, W)
    low = low_half(even.shape)
    first = jnp.where(low, even, half_turn(odd))
    second = jnp.where(low, half_turn(even), odd)
    out_ref[pl.ds(0, rows, stride=2)] = jnp.take_along_axis(first, index, axis=1, mode="promise_in_bounds")
    out_ref[pl.ds(1, rows, stride=2)] = jnp.take_along_axis(second, index, axis=1, mode="promise_in_bounds")


def place(index, narrow):
    return (index // narrow, index % narrow)


def build_maps(leaf_ref, eval_ref, leaf_map_ref, eval_map_ref):
    leaf_map_ref[...] = jnp.zeros(leaf_map_ref.shape, jnp.bfloat16)
    for c in range(2):
        for b in range(B):
            rows = pl.ds(c * 64 + b * 8, 8)
            leaf_map_ref[rows, pl.ds(b * W, W)] = leaf_ref[pl.ds(c * 8, 8)]
    row = lax.broadcasted_iota(jnp.int32, (16, W), 0)
    lane = lax.broadcasted_iota(jnp.int32, (16, W), 1)
    slot = (lane // 64) * 8 + lane % 8 == row
    for b in range(B):
        pick = jnp.where(slot & (lane % 64 // 8 == b), 1.0, 0.0).astype(jnp.bfloat16)
        block = lax.dot_general(
            eval_ref[...], pick, (((0,), (0,)), ((), ())), preferred_element_type=jnp.float32
        )
        eval_map_ref[pl.ds(b * W, W)] = block.astype(jnp.bfloat16)


def rotate(pre, cosine, sine):
    return pre * cosine + half_turn(pre) * sine


def level_map(mixing_ref, level):
    return jnp.concatenate(
        [jnp.concatenate([mixing_ref[level, j, i] for i in range(2)], axis=0) for j in range(2)], axis=1
    )


def mix(near, far, maps):
    pre = jnp.dot(jnp.concatenate([near, far], axis=1), maps, preferred_element_type=jnp.float32)
    return [pre[:, :W], pre[:, W:]]


def pair_up(even, odd):
    rows = even.shape[0]
    both = jnp.concatenate([even.reshape(rows // E, E, W), odd.reshape(rows // E, E, W)], axis=1)
    return both.reshape(2 * rows, W)


TURN_ND, FIRST_ND, LATER_PAIRS, LAST_ND = 16, 128, 4, 32
PAIRS = B // 2
ROWS = PARTS * E
EARLY = {0: 0, 1: 1, LEVELS - 1: 2}


def make_turns(me, arrived, speed_ref, phase_ref, cos_p, sin_p, cos_q, sin_q):
    terms = half_sine_terms(5)
    nd = TURN_ND
    rows = nd * E

    def body(count, _):
        arrived(count)
        step = count ^ me // nd
        at = pl.ds(pl.multiple_of(step * nd, nd), nd)
        speeds = jnp.broadcast_to(speed_ref[at], (nd, E, W)).reshape(rows, W)
        lane = lax.broadcasted_iota(jnp.int32, (rows, W), 1)
        row = lax.broadcasted_iota(jnp.int32, (rows, W), 0)
        mine = (lane // 16 == row % E) & (lane // B % 2 == me // (PARTS // 2))
        own = jnp.where(mine, speeds, 0.0)
        operand = jnp.concatenate([own + pltpu.roll(own, B, 1), own], axis=1).astype(jnp.bfloat16)
        counts = jnp.dot(operand, phase_ref[...], preferred_element_type=jnp.float32)
        low = low_half((rows, W))
        quarter = jnp.where(low, 0.0, 0.25)
        rows_at = pl.ds(pl.multiple_of(step * rows, rows), rows)
        wide_at = pl.ds(pl.multiple_of(step * rows * 2, rows * 2), rows * 2)
        for pair in range(PAIRS):
            cosine, sine, twice = [], [], []
            for b in (2 * pair, 2 * pair + 1):
                u = counts[:, b * W : (b + 1) * W] - quarter
                u = u - jnp.round(u)
                w = u * u
                p = w * jnp.float32(terms[4]) + jnp.float32(terms[3])
                for k in (2, 1, 0):
                    p = p * w + jnp.float32(terms[k])
                s = u * p
                t = 1.0 - s * s
                other = half_turn(t)
                cosine.append(jnp.where(low, t, other))
                sine.append(jnp.where(low, -other, t))
                twice.append(cosine[-1] + cosine[-1])
            last = None
            for level in range(LEVELS):
                for now, early, late in ((cosine, cos_p, cos_q), (sine, sin_p, sin_q)):
                    if level in EARLY:
                        for i in range(2):
                            early[EARLY[level], 2 * pair + i, rows_at] = now[i].astype(jnp.bfloat16)
                    else:
                        late[level - 2, pair, wide_at] = pair_up(now[0], now[1]).astype(jnp.bfloat16)
                if level == LEVELS - 1:
                    break
                if last is None:
                    after = [twice[i] * cosine[i] - 1.0 for i in range(2)], [twice[i] * sine[i] for i in range(2)]
                else:
                    after = [
                        [twice[i] * now[i] - before[i] for i in range(2)]
                        for now, before in ((cosine, last[0]), (sine, last[1]))
                    ]
                last = cosine, sine
                cosine, sine = after
        return 0

    lax.fori_loop(0, PARTS // nd, body, 0)


def first_levels(leaf_ref, leaf_map_ref, mixing_ref, cos_p, sin_p, cos_q, sin_q, state):
    nd = FIRST_ND
    rows = nd * E

    def body(step, _):
        at = pl.ds(pl.multiple_of(step * nd, nd), nd)
        rows_at = pl.ds(pl.multiple_of(step * rows, rows), rows)
        wide_at = pl.ds(pl.multiple_of(step * rows * 2, rows * 2), rows * 2)
        leaf = leaf_ref[at].reshape(rows, W)
        boxes = [None] * B
        maps = level_map(mixing_ref, 0)
        for pair in range(PAIRS):
            lanes = pl.ds(pair * 2 * W, 2 * W)
            spread = jnp.dot(leaf, leaf_map_ref[:, lanes], preferred_element_type=jnp.float32)
            pre = jnp.dot(spread.astype(jnp.bfloat16), maps, preferred_element_type=jnp.float32)
            for i in range(2):
                b = 2 * pair + i
                boxes[b] = rotate(pre[:, i * W : (i + 1) * W].astype(jnp.bfloat16), cos_p[0, b, rows_at], sin_p[0, b, rows_at])
        maps = level_map(mixing_ref, 1)
        for b in (0, 1, 4, 5):
            for i, pre in enumerate(mix(boxes[b], boxes[b + 2], maps)):
                box = b + 2 * i
                boxes[box] = rotate(pre.astype(jnp.bfloat16), cos_p[1, box, rows_at], sin_p[1, box, rows_at])
        maps = level_map(mixing_ref, 2)
        for pair in range(2):
            pres = [mix(boxes[2 * pair + i], boxes[2 * pair + i + 4], maps) for i in range(2)]
            for i in range(2):
                pre = pair_up(pres[0][i], pres[1][i]).astype(jnp.bfloat16)
                unit = pair + 2 * i
                state[unit, wide_at] = rotate(pre, cos_q[0, unit, wide_at], sin_q[0, unit, wide_at])
        return 0

    lax.fori_loop(0, PARTS // nd, body, 0)


def later_level(level, mixing_ref, cos_q, sin_q, source, target):
    stride = 2 * E << (level - 3)
    starts = range(0, 2 * ROWS, 2 * stride)

    def body(step, _):
        maps = level_map(mixing_ref, level)
        for i in range(LATER_PAIRS):
            pair = step * LATER_PAIRS + i
            near = jnp.concatenate([source[pair, pl.ds(at, stride)] for at in starts], axis=0)
            far = jnp.concatenate([source[pair, pl.ds(at + stride, stride)] for at in starts], axis=0)
            for side, pre in enumerate(mix(near, far, maps)):
                for n, at in enumerate(starts):
                    rows_at = pl.ds(at + side * stride, stride)
                    part = pre[n * stride : (n + 1) * stride].astype(jnp.bfloat16)
                    target[pair, rows_at] = rotate(
                        part, cos_q[level - 2, pair, rows_at], sin_q[level - 2, pair, rows_at]
                    )
        return 0

    lax.fori_loop(0, PAIRS // LATER_PAIRS, body, 0)


def last_level(me, send, mixing_ref, eval_map_ref, cos_p, sin_p, state, out_ref):
    level = LEVELS - 1
    nd = LAST_ND
    rows = nd * E
    steps = PARTS // 2 // nd

    def body(count, _):
        step = (count + me // nd) % steps
        maps = level_map(mixing_ref, level)
        boxes = [[], []]
        wide = [pl.ds(pl.multiple_of(step * 2 * rows + side * ROWS, 2 * rows), 2 * rows) for side in range(2)]
        for pair in range(PAIRS):
            for side, pre in enumerate(mix(state[pair, wide[0]], state[pair, wide[1]], maps)):
                own = pre.reshape(nd, 2, E, W)
                rows_at = pl.ds(pl.multiple_of(step * rows + side * (ROWS // 2), rows), rows)
                for i in range(2):
                    box = own[:, i].reshape(rows, W).astype(jnp.bfloat16)
                    at = EARLY[level], 2 * pair + i, rows_at
                    boxes[side].append(rotate(box, cos_p[at], sin_p[at]))
        for side in range(2):
            values = jnp.dot(
                jnp.concatenate(boxes[side], axis=1), eval_map_ref[...], preferred_element_type=jnp.float32
            )
            at = pl.ds(step * nd + side * (PARTS // 2), nd)
            out_ref[at] = values.astype(jnp.bfloat16).reshape(nd, E, W)

        def one(i, _):
            for side in range(2):
                send(step * nd + side * (PARTS // 2) + ((i + me) % nd))
            return 0

        lax.fori_loop(0, nd, one, 0)
        return 0

    lax.fori_loop(0, steps, body, 0)


def kernel(
    narrow, charges_hbm, order_hbm, speed_hbm, leaf_hbm, mixing_hbm, eval_hbm, phase_hbm, field,
    charges, order, speed, leaf_weight, mixing, eval_weight, phase,
    speed_rows, speeds, packed, leaf, result, leaf_map, eval_map, state, spare, cos_p, sin_p, cos_q, sin_q,
    load_sems, sends, recvs, speed_recvs, own_sem,
):
    me = lax.axis_index("wide") * narrow + lax.axis_index("narrow")
    barrier = pltpu.get_barrier_semaphore()

    def greet(k, _):
        pl.semaphore_signal(barrier, inc=1, device_id=place(me ^ k, narrow), device_id_type=MESH)
        return 0

    lax.fori_loop(1, PARTS, greet, 0)
    pairs = (
        (speed_hbm, speed), (order_hbm, order), (charges_hbm, charges), (leaf_hbm, leaf_weight),
        (eval_hbm, eval_weight), (phase_hbm, phase), (mixing_hbm, mixing),
    )
    loads = [pltpu.make_async_copy(a, b, load_sems.at[i]) for i, (a, b) in enumerate(pairs)]
    for load in loads:
        load.start()
    half = PARTS // 2
    loads[0].wait()
    speed_rows[...] = speed[...].astype(jnp.float32).reshape(half, 1, W)
    loads[1].wait()
    loads[2].wait()
    pack_rows(charges, order, packed)
    loads[3].wait()
    loads[4].wait()
    build_maps(leaf_weight, eval_weight, leaf_map, eval_map)
    pl.semaphore_wait(barrier, PARTS - 1)

    def remote(source, target, i, to, recv):
        return pltpu.make_async_remote_copy(
            source, target.at[me], sends.at[i], recv, device_id=place(to, narrow), device_id_type=MESH
        )

    def send_speed(k, _):
        to = me ^ k
        remote(speed_rows.at[to % half], speeds, 0, to, speed_recvs.at[k // TURN_ND]).start()
        return 0

    def send_leaf(k, _):
        to = me ^ k
        remote(packed.at[to], leaf, 1, to, recvs.at[0]).start()
        return 0

    lax.fori_loop(1, PARTS, send_speed, 0)
    lax.fori_loop(1, PARTS, send_leaf, 0)
    speeds[me] = speed_rows[me % half]
    leaf[me] = packed[me]

    def wait(ref, sem, count=PARTS - 1):
        some = pl.ds(0, count)
        pltpu.make_async_copy(ref.at[some], ref.at[some], sem).wait()

    def arrived(count):
        @pl.when(count == 0)
        def _():
            wait(speeds, speed_recvs.at[count], TURN_ND - 1)

        @pl.when(count > 0)
        def _():
            wait(speeds, speed_recvs.at[count], TURN_ND)

    loads[5].wait()
    make_turns(me, arrived, speeds, phase, cos_p, sin_p, cos_q, sin_q)
    loads[6].wait()
    wait(leaf, recvs.at[0])
    first_levels(leaf, leaf_map, mixing, cos_p, sin_p, cos_q, sin_q, state)
    now, later = state, spare
    for level in range(3, LEVELS - 1):
        later_level(level, mixing, cos_q, sin_q, now, later)
        now, later = later, now

    def send_result(to):
        @pl.when(to != me)
        def _():
            remote(result.at[to], field, 2, to, recvs.at[1]).start()

    last_level(me, send_result, mixing, eval_map, cos_p, sin_p, now, result)
    own = pltpu.make_async_copy(result.at[me], field.at[me], own_sem)
    own.start()
    wait(speeds, sends.at[0])
    wait(packed, sends.at[1])
    wait(result, recvs.at[1])
    wait(result, sends.at[2])
    own.wait()


def on_device(narrow, charges, source_order, velocity, leaf_weight, mixing, eval_weight, target_order):
    lines = charges.shape[1] // W
    half = PARTS // 2
    args = (
        charges.reshape(2, lines, W).transpose(1, 0, 2).reshape(2 * lines, W),
        source_order.reshape(lines, W),
        velocity.reshape(half, W),
        leaf_weight,
        mixing,
        eval_weight.T,
        jnp.asarray(phase_map()),
    )
    chunk = pltpu.VMEM((PARTS, E, W), jnp.bfloat16)
    states = pltpu.VMEM((PAIRS, 2 * ROWS, W), jnp.bfloat16)
    field = pl.pallas_call(
        functools.partial(kernel, narrow),
        out_shape=jax.ShapeDtypeStruct((PARTS, E, W), jnp.bfloat16),
        in_specs=[pl.BlockSpec(memory_space=pltpu.HBM)] * len(args),
        out_specs=pl.BlockSpec(memory_space=pltpu.HBM),
        scratch_shapes=[pltpu.VMEM(a.shape, a.dtype) for a in args]
        + [
            pltpu.VMEM((half, 1, W), jnp.float32),
            pltpu.VMEM((PARTS, 1, W), jnp.float32),
            chunk,
            chunk,
            chunk,
            pltpu.VMEM((W, B * W), jnp.bfloat16),
            pltpu.VMEM((B * W, W), jnp.bfloat16),
            states,
            states,
            pltpu.VMEM((len(EARLY), B, ROWS, W), jnp.bfloat16),
            pltpu.VMEM((len(EARLY), B, ROWS, W), jnp.bfloat16),
            pltpu.VMEM((LEVELS - len(EARLY), PAIRS, 2 * ROWS, W), jnp.bfloat16),
            pltpu.VMEM((LEVELS - len(EARLY), PAIRS, 2 * ROWS, W), jnp.bfloat16),
            pltpu.SemaphoreType.DMA((len(args),)),
            pltpu.SemaphoreType.DMA((3,)),
            pltpu.SemaphoreType.DMA((2,)),
            pltpu.SemaphoreType.DMA((PARTS // TURN_ND,)),
            pltpu.SemaphoreType.DMA,
        ],
        compiler_params=pltpu.CompilerParams(
            has_side_effects=True, collective_id=0, vmem_limit_bytes=62 * 2**20
        ),
    )(*args)
    blocks = 2
    out = pl.pallas_call(
        unpack_kernel,
        grid=(blocks,),
        out_shape=jax.ShapeDtypeStruct((2 * lines, W), jnp.float32),
        in_specs=[
            pl.BlockSpec((2, half // blocks, E, W), lambda i: (0, i, 0, 0)),
            pl.BlockSpec((lines // blocks, W), lambda i: (i, 0)),
        ],
        out_specs=pl.BlockSpec((2 * lines // blocks, W), lambda i: (i, 0)),
    )(field.reshape(2, half, E, W), target_order.reshape(lines, W))
    return out.reshape(lines, 2, W).transpose(1, 0, 2).reshape(2, lines * W)


def solution(mesh):
    both = ("wide", "narrow")
    return jax.shard_map(
        functools.partial(on_device, mesh.shape["narrow"]),
        mesh=mesh,
        in_specs=(P(None, both), P(both), P(both), P(), P(), P(), P(both)),
        out_specs=P(None, both),
        check_vma=False,
    )
```

```python
import functools
import math

import jax
import jax.numpy as jnp
import numpy as np
from jax import lax
from jax.experimental import pallas as pl
from jax.experimental.pallas import tpu as pltpu
from jax.sharding import PartitionSpec as P

MESH = pl.DeviceIdType.MESH
LEVELS = 10
PARTS = 128
E = 8
B = 8
W = 128


def half_sine_terms(count):
    w = 0.125 * (1 + np.cos(np.pi * (np.arange(64) + 0.5) / 64))
    u = np.sqrt(w)
    target = math.sqrt(2) * np.sin(np.pi * u) / u
    return np.polynomial.polynomial.polyfit(w, target, count - 1)


def phase_map():
    rank = W // 2
    nodes = np.cos(np.float32(math.pi) * (np.arange(rank, dtype=np.float32) + np.float32(0.5)) / np.float32(rank))
    rest = np.tile(nodes.astype(np.float64) * 0.5, 2)
    pieces = []
    for _ in range(3):
        pieces.append(rest.astype(jnp.bfloat16).astype(np.float64))
        rest = rest - pieces[-1]
    out = np.zeros((2, E, 2, B, B, W), np.float64)
    for b in range(B):
        out[0, :, 0, b, b, :] = pieces[0]
        out[0, :, 1, b, b, :] = pieces[1]
        out[1, :, :, b, b, :] = pieces[2]
    return out.reshape(2 * W, B * W).astype(jnp.bfloat16)


def low_half(shape):
    return lax.broadcasted_iota(jnp.int32, shape, len(shape) - 1) % W < W // 2


def half_turn(x):
    return pltpu.roll(x, W // 2, x.ndim - 1)


def slot_of(order):
    lane = lax.broadcasted_iota(jnp.int32, order.shape, 1)
    return (lane // 8) * 8 + order


def pack_rows(charges_ref, order_ref, out_ref):
    rows = 64
    half = PARTS // 2

    def body(step, _):
        at = pl.ds(pl.multiple_of(step * rows, rows), rows)
        index = slot_of(order_ref[at])
        first = charges_ref[pl.ds(pl.multiple_of(step * 2 * rows, 2 * rows), rows, stride=2)]
        second = charges_ref[pl.ds(step * 2 * rows + 1, rows, stride=2)]
        first = jnp.take_along_axis(first, index, axis=1, mode="promise_in_bounds")
        second = jnp.take_along_axis(second, index, axis=1, mode="promise_in_bounds")
        low = low_half(first.shape)
        even = jnp.where(low, first, half_turn(second)).astype(jnp.bfloat16)
        odd = jnp.where(low, half_turn(first), second).astype(jnp.bfloat16)
        out_ref[pl.ds(step * (rows // E), rows // E)] = even.reshape(rows // E, E, W)
        out_ref[pl.ds(half + step * (rows // E), rows // E)] = odd.reshape(rows // E, E, W)
        return 0

    lax.fori_loop(0, half * E // rows, body, 0)


def unpack_kernel(field_ref, order_ref, out_ref):
    rows = order_ref.shape[0]
    index = slot_of(order_ref[...])
    even = field_ref[0].astype(jnp.float32).reshape(rows, W)
    odd = field_ref[1].astype(jnp.float32).reshape(rows, W)
    low = low_half(even.shape)
    first = jnp.where(low, even, half_turn(odd))
    second = jnp.where(low, half_turn(even), odd)
    out_ref[pl.ds(0, rows, stride=2)] = jnp.take_along_axis(first, index, axis=1, mode="promise_in_bounds")
    out_ref[pl.ds(1, rows, stride=2)] = jnp.take_along_axis(second, index, axis=1, mode="promise_in_bounds")


def place(index, narrow):
    return (index // narrow, index % narrow)


def build_maps(leaf_ref, eval_ref, leaf_map_ref, eval_map_ref):
    leaf_map_ref[...] = jnp.zeros(leaf_map_ref.shape, jnp.bfloat16)
    for c in range(2):
        for b in range(B):
            rows = pl.ds(c * 64 + b * 8, 8)
            leaf_map_ref[rows, pl.ds(b * W, W)] = leaf_ref[pl.ds(c * 8, 8)]
    row = lax.broadcasted_iota(jnp.int32, (16, W), 0)
    lane = lax.broadcasted_iota(jnp.int32, (16, W), 1)
    slot = (lane // 64) * 8 + lane % 8 == row
    for b in range(B):
        pick = jnp.where(slot & (lane % 64 // 8 == b), 1.0, 0.0).astype(jnp.bfloat16)
        block = lax.dot_general(
            eval_ref[...], pick, (((0,), (0,)), ((), ())), preferred_element_type=jnp.float32
        )
        eval_map_ref[pl.ds(b * W, W)] = block.astype(jnp.bfloat16)


def rotate(pre, cosine, sine):
    return pre * cosine + half_turn(pre) * sine


def level_map(mixing_ref, level):
    return jnp.concatenate(
        [jnp.concatenate([mixing_ref[level, j, i] for i in range(2)], axis=0) for j in range(2)], axis=1
    )


def mix(near, far, maps):
    pre = jnp.dot(jnp.concatenate([near, far], axis=1), maps, preferred_element_type=jnp.float32)
    return [pre[:, :W], pre[:, W:]]


def pair_up(even, odd):
    rows = even.shape[0]
    both = jnp.concatenate([even.reshape(rows // E, E, W), odd.reshape(rows // E, E, W)], axis=1)
    return both.reshape(2 * rows, W)


TURN_ND, FIRST_ND, LATER_PAIRS, LAST_ND = 32, 128, 4, 32
PAIRS = B // 2
ROWS = PARTS * E
EARLY = {0: 0, 1: 1, LEVELS - 1: 2}


def make_turns(me, arrived, speed_ref, phase_ref, cos_p, sin_p, cos_q, sin_q):
    terms = half_sine_terms(5)
    nd = TURN_ND
    rows = nd * E

    def body(count, _):
        arrived(count)
        step = count ^ me // nd
        at = pl.ds(pl.multiple_of(step * nd, nd), nd)
        speeds = jnp.broadcast_to(speed_ref[at], (nd, E, W)).reshape(rows, W)
        lane = lax.broadcasted_iota(jnp.int32, (rows, W), 1)
        row = lax.broadcasted_iota(jnp.int32, (rows, W), 0)
        mine = (lane // 16 == row % E) & (lane // B % 2 == me // (PARTS // 2))
        own = jnp.where(mine, speeds, 0.0)
        operand = jnp.concatenate([own + pltpu.roll(own, B, 1), own], axis=1).astype(jnp.bfloat16)
        counts = jnp.dot(operand, phase_ref[...], preferred_element_type=jnp.float32)
        low = low_half((rows, W))
        quarter = jnp.where(low, 0.0, 0.25)
        rows_at = pl.ds(pl.multiple_of(step * rows, rows), rows)
        wide_at = pl.ds(pl.multiple_of(step * rows * 2, rows * 2), rows * 2)
        for pair in range(PAIRS):
            cosine, sine, twice = [], [], []
            for b in (2 * pair, 2 * pair + 1):
                u = counts[:, b * W : (b + 1) * W] - quarter
                u = u - jnp.round(u)
                w = u * u
                p = w * jnp.float32(terms[4]) + jnp.float32(terms[3])
                for k in (2, 1, 0):
                    p = p * w + jnp.float32(terms[k])
                s = u * p
                t = 1.0 - s * s
                other = half_turn(t)
                cosine.append(jnp.where(low, t, other))
                sine.append(jnp.where(low, -other, t))
                twice.append(cosine[-1] + cosine[-1])
            last = None
            for level in range(LEVELS):
                for now, early, late in ((cosine, cos_p, cos_q), (sine, sin_p, sin_q)):
                    if level in EARLY:
                        for i in range(2):
                            early[EARLY[level], 2 * pair + i, rows_at] = now[i].astype(jnp.bfloat16)
                    else:
                        late[level - 2, pair, wide_at] = pair_up(now[0], now[1]).astype(jnp.bfloat16)
                if level == LEVELS - 1:
                    break
                if last is None:
                    after = [twice[i] * cosine[i] - 1.0 for i in range(2)], [twice[i] * sine[i] for i in range(2)]
                else:
                    after = [
                        [twice[i] * now[i] - before[i] for i in range(2)]
                        for now, before in ((cosine, last[0]), (sine, last[1]))
                    ]
                last = cosine, sine
                cosine, sine = after
        return 0

    lax.fori_loop(0, PARTS // nd, body, 0)


def first_levels(leaf_ref, leaf_map_ref, mixing_ref, cos_p, sin_p, cos_q, sin_q, state):
    nd = FIRST_ND
    rows = nd * E

    def body(step, _):
        at = pl.ds(pl.multiple_of(step * nd, nd), nd)
        rows_at = pl.ds(pl.multiple_of(step * rows, rows), rows)
        wide_at = pl.ds(pl.multiple_of(step * rows * 2, rows * 2), rows * 2)
        leaf = leaf_ref[at].reshape(rows, W)
        boxes = [None] * B
        maps = level_map(mixing_ref, 0)
        for pair in range(PAIRS):
            lanes = pl.ds(pair * 2 * W, 2 * W)
            spread = jnp.dot(leaf, leaf_map_ref[:, lanes], preferred_element_type=jnp.float32)
            pre = jnp.dot(spread.astype(jnp.bfloat16), maps, preferred_element_type=jnp.float32)
            for i in range(2):
                b = 2 * pair + i
                boxes[b] = rotate(pre[:, i * W : (i + 1) * W].astype(jnp.bfloat16), cos_p[0, b, rows_at], sin_p[0, b, rows_at])
        maps = level_map(mixing_ref, 1)
        for b in (0, 1, 4, 5):
            for i, pre in enumerate(mix(boxes[b], boxes[b + 2], maps)):
                box = b + 2 * i
                boxes[box] = rotate(pre.astype(jnp.bfloat16), cos_p[1, box, rows_at], sin_p[1, box, rows_at])
        maps = level_map(mixing_ref, 2)
        for pair in range(2):
            pres = [mix(boxes[2 * pair + i], boxes[2 * pair + i + 4], maps) for i in range(2)]
            for i in range(2):
                pre = pair_up(pres[0][i], pres[1][i]).astype(jnp.bfloat16)
                unit = pair + 2 * i
                state[unit, wide_at] = rotate(pre, cos_q[0, unit, wide_at], sin_q[0, unit, wide_at])
        return 0

    lax.fori_loop(0, PARTS // nd, body, 0)


def later_level(level, mixing_ref, cos_q, sin_q, source, target):
    stride = 2 * E << (level - 3)
    starts = range(0, 2 * ROWS, 2 * stride)

    def body(step, _):
        maps = level_map(mixing_ref, level)
        for i in range(LATER_PAIRS):
            pair = step * LATER_PAIRS + i
            near = jnp.concatenate([source[pair, pl.ds(at, stride)] for at in starts], axis=0)
            far = jnp.concatenate([source[pair, pl.ds(at + stride, stride)] for at in starts], axis=0)
            for side, pre in enumerate(mix(near, far, maps)):
                for n, at in enumerate(starts):
                    rows_at = pl.ds(at + side * stride, stride)
                    part = pre[n * stride : (n + 1) * stride].astype(jnp.bfloat16)
                    target[pair, rows_at] = rotate(
                        part, cos_q[level - 2, pair, rows_at], sin_q[level - 2, pair, rows_at]
                    )
        return 0

    lax.fori_loop(0, PAIRS // LATER_PAIRS, body, 0)


def last_level(me, send, mixing_ref, eval_map_ref, cos_p, sin_p, state, out_ref):
    level = LEVELS - 1
    nd = LAST_ND
    rows = nd * E
    steps = PARTS // 2 // nd

    def body(count, _):
        step = (count + me // nd) % steps
        maps = level_map(mixing_ref, level)
        boxes = [[], []]
        wide = [pl.ds(pl.multiple_of(step * 2 * rows + side * ROWS, 2 * rows), 2 * rows) for side in range(2)]
        for pair in range(PAIRS):
            for side, pre in enumerate(mix(state[pair, wide[0]], state[pair, wide[1]], maps)):
                own = pre.reshape(nd, 2, E, W)
                rows_at = pl.ds(pl.multiple_of(step * rows + side * (ROWS // 2), rows), rows)
                for i in range(2):
                    box = own[:, i].reshape(rows, W).astype(jnp.bfloat16)
                    at = EARLY[level], 2 * pair + i, rows_at
                    boxes[side].append(rotate(box, cos_p[at], sin_p[at]))
        for side in range(2):
            values = jnp.dot(
                jnp.concatenate(boxes[side], axis=1), eval_map_ref[...], preferred_element_type=jnp.float32
            )
            at = pl.ds(step * nd + side * (PARTS // 2), nd)
            out_ref[at] = values.astype(jnp.bfloat16).reshape(nd, E, W)

        def one(i, _):
            for side in range(2):
                send(step * nd + side * (PARTS // 2) + ((i + me) % nd))
            return 0

        lax.fori_loop(0, nd, one, 0)
        return 0

    lax.fori_loop(0, steps, body, 0)


def kernel(
    narrow, charges_hbm, order_hbm, speed_hbm, leaf_hbm, mixing_hbm, eval_hbm, phase_hbm, field,
    charges, order, speed, leaf_weight, mixing, eval_weight, phase,
    speed_rows, speeds, packed, leaf, result, leaf_map, eval_map, state, spare, cos_p, sin_p, cos_q, sin_q,
    load_sems, sends, recvs, speed_recvs, own_sem,
):
    me = lax.axis_index("wide") * narrow + lax.axis_index("narrow")
    barrier = pltpu.get_barrier_semaphore()

    def greet(k, _):
        pl.semaphore_signal(barrier, inc=1, device_id=place(me ^ k, narrow), device_id_type=MESH)
        return 0

    lax.fori_loop(1, PARTS, greet, 0)
    pairs = (
        (speed_hbm, speed), (order_hbm, order), (charges_hbm, charges), (leaf_hbm, leaf_weight),
        (eval_hbm, eval_weight), (phase_hbm, phase), (mixing_hbm, mixing),
    )
    loads = [pltpu.make_async_copy(a, b, load_sems.at[i]) for i, (a, b) in enumerate(pairs)]
    for load in loads:
        load.start()
    half = PARTS // 2
    loads[0].wait()
    speed_rows[...] = speed[...].astype(jnp.float32).reshape(half, 1, W)
    loads[1].wait()
    loads[2].wait()
    pack_rows(charges, order, packed)
    loads[3].wait()
    loads[4].wait()
    build_maps(leaf_weight, eval_weight, leaf_map, eval_map)
    pl.semaphore_wait(barrier, PARTS - 1)

    def remote(source, target, i, to, recv):
        return pltpu.make_async_remote_copy(
            source, target.at[me], sends.at[i], recv, device_id=place(to, narrow), device_id_type=MESH
        )

    def send_speed(k, _):
        to = me ^ k
        remote(speed_rows.at[to % half], speeds, 0, to, speed_recvs.at[k // TURN_ND]).start()
        return 0

    def send_leaf(k, _):
        to = me ^ k
        remote(packed.at[to], leaf, 1, to, recvs.at[0]).start()
        return 0

    lax.fori_loop(1, PARTS, send_speed, 0)
    lax.fori_loop(1, PARTS, send_leaf, 0)
    speeds[me] = speed_rows[me % half]
    leaf[me] = packed[me]

    def wait(ref, sem, count=PARTS - 1):
        some = pl.ds(0, count)
        pltpu.make_async_copy(ref.at[some], ref.at[some], sem).wait()

    def arrived(count):
        @pl.when(count == 0)
        def _():
            wait(speeds, speed_recvs.at[count], TURN_ND - 1)

        @pl.when(count > 0)
        def _():
            wait(speeds, speed_recvs.at[count], TURN_ND)

    loads[5].wait()
    make_turns(me, arrived, speeds, phase, cos_p, sin_p, cos_q, sin_q)
    loads[6].wait()
    wait(leaf, recvs.at[0])
    first_levels(leaf, leaf_map, mixing, cos_p, sin_p, cos_q, sin_q, state)
    now, later = state, spare
    for level in range(3, LEVELS - 1):
        later_level(level, mixing, cos_q, sin_q, now, later)
        now, later = later, now

    def send_result(to):
        @pl.when(to != me)
        def _():
            remote(result.at[to], field, 2, to, recvs.at[1]).start()

    last_level(me, send_result, mixing, eval_map, cos_p, sin_p, now, result)
    own = pltpu.make_async_copy(result.at[me], field.at[me], own_sem)
    own.start()
    wait(speeds, sends.at[0])
    wait(packed, sends.at[1])
    wait(result, recvs.at[1])
    wait(result, sends.at[2])
    own.wait()


def on_device(narrow, charges, source_order, velocity, leaf_weight, mixing, eval_weight, target_order):
    lines = charges.shape[1] // W
    half = PARTS // 2
    args = (
        charges.reshape(2, lines, W).transpose(1, 0, 2).reshape(2 * lines, W),
        source_order.reshape(lines, W),
        velocity.reshape(half, W),
        leaf_weight,
        mixing,
        eval_weight.T,
        jnp.asarray(phase_map()),
    )
    chunk = pltpu.VMEM((PARTS, E, W), jnp.bfloat16)
    states = pltpu.VMEM((PAIRS, 2 * ROWS, W), jnp.bfloat16)
    field = pl.pallas_call(
        functools.partial(kernel, narrow),
        out_shape=jax.ShapeDtypeStruct((PARTS, E, W), jnp.bfloat16),
        in_specs=[pl.BlockSpec(memory_space=pltpu.HBM)] * len(args),
        out_specs=pl.BlockSpec(memory_space=pltpu.HBM),
        scratch_shapes=[pltpu.VMEM(a.shape, a.dtype) for a in args]
        + [
            pltpu.VMEM((half, 1, W), jnp.float32),
            pltpu.VMEM((PARTS, 1, W), jnp.float32),
            chunk,
            chunk,
            chunk,
            pltpu.VMEM((W, B * W), jnp.bfloat16),
            pltpu.VMEM((B * W, W), jnp.bfloat16),
            states,
            states,
            pltpu.VMEM((len(EARLY), B, ROWS, W), jnp.bfloat16),
            pltpu.VMEM((len(EARLY), B, ROWS, W), jnp.bfloat16),
            pltpu.VMEM((LEVELS - len(EARLY), PAIRS, 2 * ROWS, W), jnp.bfloat16),
            pltpu.VMEM((LEVELS - len(EARLY), PAIRS, 2 * ROWS, W), jnp.bfloat16),
            pltpu.SemaphoreType.DMA((len(args),)),
            pltpu.SemaphoreType.DMA((3,)),
            pltpu.SemaphoreType.DMA((2,)),
            pltpu.SemaphoreType.DMA((PARTS // TURN_ND,)),
            pltpu.SemaphoreType.DMA,
        ],
        compiler_params=pltpu.CompilerParams(
            has_side_effects=True, collective_id=0, vmem_limit_bytes=62 * 2**20
        ),
    )(*args)
    blocks = 2
    out = pl.pallas_call(
        unpack_kernel,
        grid=(blocks,),
        out_shape=jax.ShapeDtypeStruct((2 * lines, W), jnp.float32),
        in_specs=[
            pl.BlockSpec((2, half // blocks, E, W), lambda i: (0, i, 0, 0)),
            pl.BlockSpec((lines // blocks, W), lambda i: (i, 0)),
        ],
        out_specs=pl.BlockSpec((2 * lines // blocks, W), lambda i: (i, 0)),
    )(field.reshape(2, half, E, W), target_order.reshape(lines, W))
    return out.reshape(lines, 2, W).transpose(1, 0, 2).reshape(2, lines * W)


def solution(mesh):
    both = ("wide", "narrow")
    return jax.shard_map(
        functools.partial(on_device, mesh.shape["narrow"]),
        mesh=mesh,
        in_specs=(P(None, both), P(both), P(both), P(), P(), P(), P(both)),
        out_specs=P(None, both),
        check_vma=False,
    )
```
